32 devices in a mesh: fsdp: 8 (over y, x, core), sp: 4 (over z).
Axes of the slice: x: 2, y: 2, z: 4, core: 2. Of those that a mesh axis runs over, the one named last changes fastest.
Arguments:
- inputs: bfloat16 [16, 1024, 768], P('fsdp', 'sp'), may hold values from -6 to 6
- block_ids: int32 [16, 1024], P('fsdp', 'sp'), may hold values from 0 to 3, never falling along the last dimension, each value on 1 to 512 neighbouring positions
- first_gain: bfloat16 [768], P('fsdp'), may hold values from 0.5 to 1.5
- first_shift: bfloat16 [768], P('fsdp'), may hold values from -3 to 3
- w_project: bfloat16 [768, 2304], P('fsdp'), may hold values from -0.21875 to 0.21875
- query_bias: bfloat16 [768], P('fsdp'), may hold values from -3 to 3
- value_bias: bfloat16 [768], P('fsdp'), may hold values from -3 to 3
- w_output: bfloat16 [768, 768], P('fsdp'), may hold values from -4 to 4
- output_bias: bfloat16 [768], P('fsdp'), may hold values from -3 to 3
- second_gain: bfloat16 [768], P('fsdp'), may hold values from 0.5 to 1.5
- second_shift: bfloat16 [768], P('fsdp'), may hold values from -3 to 3
- w_expand: bfloat16 [768, 3072], P('fsdp'), may hold values from -0.21875 to 0.21875
- expand_bias: bfloat16 [3072], P('fsdp'), may hold values from -3 to 3
- w_reduce: bfloat16 [3072, 768], P('fsdp'), may hold values from -0.109375 to 0.109375
- reduce_bias: bfloat16 [768], P('fsdp'), may hold values from -3 to 3
- out_grad: bfloat16 [16, 1024, 768], P('fsdp', 'sp'), may hold values from -6 to 6
Outputs:
- layer_output: bfloat16 [16, 1024, 768], P('fsdp', 'sp')
- input_grad: float32 [16, 1024, 768], P('fsdp', 'sp')
- grad_first_gain: float32 [768], P('fsdp')
- grad_first_shift: float32 [768], P('fsdp')
- grad_project: float32 [768, 2304], P('fsdp')
- grad_query_bias: float32 [768], P('fsdp')
- grad_value_bias: float32 [768], P('fsdp')
- grad_output: float32 [768, 768], P('fsdp')
- grad_output_bias: float32 [768], P('fsdp')
- grad_second_gain: float32 [768], P('fsdp')
- grad_second_shift: float32 [768], P('fsdp')
- grad_expand: float32 [768, 3072], P('fsdp')
- grad_expand_bias: float32 [3072], P('fsdp')
- grad_reduce: float32 [3072, 768], P('fsdp')
- grad_reduce_bias: float32 [768], P('fsdp')
The draws below stay inside these ranges and needn't reach their ends.
Inputs may be any that keep to these rules, and one draw needn't show every extreme that they name: `block_ids`: block numbers never fall along a sequence, and every number from 0 to 3 occurs in each sequence.
All inputs are finite; a program needn't handle non-finite values.
Results may differ from the reference program's by a relative error of at most 0.011.
Values may be sent and summed in bfloat16 or wider, within the bound.
No kernel may reach another device: no remote copies, remote signals or barrier semaphores. Data moves between devices by JAX's collectives and lax.ppermute only.
A program may use at most 192 MiB of HBM per device.

```python
import math
import jax
import jax.numpy as jnp
import numpy as np
from jax import lax

D = 768
H = 12
HD = 64
FF = 3072
LEN = 1024
NBLK = 4
SEQS = 16


def spiked(entries, key, source, target, shards_of, factor):
    owner, partner = [(jnp.arange(entries.shape[axis_at]) // (entries.shape[axis_at] // shards_of)).reshape([-1 if axis == axis_at else 1 for axis in range(entries.ndim)]) for axis_at in (source, target)]
    chosen = jax.random.permutation(key, shards_of)[partner]
    strong = (owner == chosen) | (owner == (partner + shards_of // 2) % shards_of)
    return jnp.where(strong, factor * entries, entries)


def level_of(stream_key, dims, cuts, least, largest):
    level, own = 1.0, jax.random.fold_in(stream_key, 6)
    for position, shards_of in cuts:
        draws = jnp.exp(jax.random.uniform(jax.random.fold_in(own, position), (shards_of,), jnp.float32, least / len(cuts), largest / len(cuts)))
        level = level * jnp.repeat(draws, dims[position] // shards_of).reshape([-1 if axis == position else 1 for axis in range(len(dims))])
    return level


def split_up(number_of, total, bound, slope):
    weights = [(1 << 20) // math.isqrt(grade ** slope) + 1 for grade in range(2, number_of + 1)]
    rest, counts = total - bound - (number_of - 1), [1] * (number_of - 1)
    while rest > 0:
        candidates = [i for i in range(number_of - 1) if counts[i] < bound]
        mass, budget = sum([weights[i] for i in candidates]), rest
        for i in candidates:
            more = min(bound - counts[i], max(1, budget * weights[i] // mass), rest)
            counts[i] = counts[i] + more
            rest = rest - more
    return np.array([bound] + counts)


def uneven_parts(stream_key, number_of, total, reach, lean):
    if number_of == 2:
        one = jax.random.randint(stream_key, (), max(1, total - reach), min(reach, total - 1) + 1)
        return jnp.stack([one, total - one])
    sizes = jnp.asarray(split_up(number_of, total, reach, lean), jnp.int32)
    pairs = (number_of - 1) // 2
    source_of, sink = sizes[1:1 + 2 * pairs:2], sizes[2:2 + 2 * pairs:2]
    margin = jnp.minimum(source_of - 1, reach - sink)
    shifted = jax.random.randint(jax.random.fold_in(stream_key, 1), (pairs,), 0, 1 << 20) % (margin + 1)
    sizes = sizes.at[1:1 + 2 * pairs:2].set(source_of - shifted).at[2:2 + 2 * pairs:2].set(sink + shifted)
    return sizes[jax.random.permutation(jax.random.fold_in(stream_key, 2), number_of)]


def centred(stream_key, extent, scale, most, cuts=(), kind=jnp.bfloat16):
    array = scale * jax.random.normal(stream_key, extent, jnp.float32)
    if cuts:
        array = array * level_of(stream_key, extent, cuts, -0.22, 0.18)
    return jnp.clip(array, -most, most).astype(kind)


def gaussian_with(stream_key, dims, scale, bound, pieces, heavy, dtype=jnp.bfloat16):
    drawn = scale * jax.random.normal(stream_key, dims, jnp.float32)
    if pieces:
        drawn = drawn * level_of(stream_key, dims, pieces, -0.22, 0.18)
    return jnp.clip(spiked(drawn, jax.random.fold_in(stream_key, 3), *heavy), -bound, bound).astype(dtype)


def setup_inputs(seed: int = 0) -> dict:
    streams_of = jax.random.split(jax.random.key(seed), 17)
    return {
        "inputs": gaussian_with(streams_of[0], (SEQS, LEN, D), 1.0, 6.0, ((0, 8), (1, 4)), (0, 2, 8, 2.0)),
        "block_ids": jax.vmap(lambda own: jnp.searchsorted(jnp.cumsum(uneven_parts(own, NBLK, LEN, LEN // 2, 1)), jnp.arange(LEN), side="right"))(jax.random.split(streams_of[1], SEQS)).reshape((SEQS, LEN)).astype(jnp.int32),
        "first_gain": jnp.clip(1.0 + 0.1 * jax.random.normal(streams_of[2], (D,), jnp.float32), 0.5, 1.5).astype(jnp.bfloat16),
        "first_shift": centred(streams_of[3], (D,), 0.5, 3.0, ((0, 8),)),
        "w_project": centred(streams_of[4], (D, 3 * D), D ** -0.5, 0.21875, ((0, 8),)),
        "query_bias": centred(streams_of[5], (D,), 0.5, 3.0, ((0, 8),)),
        "value_bias": centred(streams_of[6], (D,), 0.5, 3.0, ((0, 8),)),
        "w_output": centred(streams_of[7], (D, D), (max(D // 384, 2)) ** -0.5, 4.0, ((0, 8),)),
        "output_bias": centred(streams_of[8], (D,), 0.5, 3.0, ((0, 8),)),
        "second_gain": jnp.clip(1.0 + 0.1 * jax.random.normal(streams_of[9], (D,), jnp.float32), 0.5, 1.5).astype(jnp.bfloat16),
        "second_shift": centred(streams_of[10], (D,), 0.5, 3.0, ((0, 8),)),
        "w_expand": centred(streams_of[11], (D, FF), D ** -0.5, 0.21875, ((0, 8),)),
        "expand_bias": centred(streams_of[12], (FF,), 0.5, 3.0, ((0, 8),)),
        "w_reduce": centred(streams_of[13], (FF, D), FF ** -0.5, 0.109375, ((0, 8),)),
        "reduce_bias": centred(streams_of[14], (D,), 0.5, 3.0, ((0, 8),)),
        "out_grad": gaussian_with(streams_of[15], (SEQS, LEN, D), 1.0, 6.0, ((0, 8), (1, 4)), (0, 2, 8, 2.0)),
    }


EPSILON = 1e-05
GELU_C = 0.7978845608028654
GELU_A = 0.044715
MASKED = -1e+30

@jax.custom_vjp
def low(v):
    return lax.optimization_barrier(v.astype(jnp.bfloat16)).astype(jnp.float32)

@jax.custom_vjp
def low_back(v):
    return v

def low_keep(v):
    return (low(v), None)

def low_pass(kept, grad):
    return (grad,)

def back_keep(v):
    return (v, None)

def back_low(kept, grad):
    return (low(grad),)
low.defvjp(low_keep, low_pass)
low_back.defvjp(back_keep, back_low)

def layer_norm(rows, gain, shift):
    average = lax.optimization_barrier(jnp.mean(rows, axis=-1, keepdims=True))
    centered = rows - average
    variance = lax.optimization_barrier(jnp.mean(centered * centered, axis=-1, keepdims=True))
    return centered * lax.rsqrt(variance + EPSILON) * gain + shift

def gelu_tanh(pre):
    return 0.5 * pre * (1.0 + jnp.tanh(GELU_C * (pre + GELU_A * pre * pre * pre)))

def product(form, left, right):
    return jnp.einsum(form, left, right, precision=lax.Precision.HIGHEST)

def forward(params, inputs, blocks):
    gain_one, shift_one, w_proj, q_bias, v_bias, w_out, out_bias, gain_two, shift_two, w_exp, exp_bias, w_red, red_bias = params
    groups, length, width = inputs.shape
    normed_in = low(layer_norm(inputs, gain_one, shift_one))
    bias_all = jnp.concatenate([q_bias, jnp.zeros_like(q_bias), v_bias])
    projected = low_back(low(product('gld,de->gle', normed_in, w_proj) + bias_all))
    split = projected.reshape(groups, length, 3, H, HD)
    queries = jnp.transpose(split[:, :, 0], (2, 0, 1, 3))
    keys_all = jnp.transpose(split[:, :, 1], (2, 0, 1, 3))
    values_all = jnp.transpose(split[:, :, 2], (2, 0, 1, 3))
    allowed = blocks[:, None, :] <= blocks[:, :, None]
    scale = 1.0 / math.sqrt(HD)

    def one_head(item):
        query, keys, values = item
        scores = low_back(product('gqd,gkd->gqk', query, keys) * scale)
        scores = jnp.where(allowed, scores, MASKED)
        peak = lax.optimization_barrier(jnp.max(scores, axis=-1, keepdims=True))
        raised = jnp.exp(scores - peak)
        attn_prob = low(raised / lax.optimization_barrier(jnp.sum(raised, axis=-1, keepdims=True)))
        return product('gqk,gkd->gqd', attn_prob, values)
    mixed = low_back(low(lax.map(jax.checkpoint(one_head), (queries, keys_all, values_all))))
    attended = jnp.transpose(mixed, (1, 2, 0, 3)).reshape(groups, length, width)
    middle = inputs + low_back(product('gld,de->gle', attended, w_out) + out_bias)
    normed_mid = low(layer_norm(middle, gain_two, shift_two))
    hidden = low_back(product('gld,df->glf', normed_mid, w_exp) + exp_bias)
    active = low(gelu_tanh(hidden))
    return middle + (product('glf,fd->gld', active, w_red) + red_bias)

def reference(inputs, block_ids, first_gain, first_shift, w_project, query_bias, value_bias, w_output, output_bias, second_gain, second_shift, w_expand, expand_bias, w_reduce, reduce_bias, out_grad):
    params = tuple((value.astype(jnp.float32) for value in (first_gain, first_shift, w_project, query_bias, value_bias, w_output, output_bias, second_gain, second_shift, w_expand, expand_bias, w_reduce, reduce_bias)))
    group = 4 if SEQS % 4 == 0 else 1
    count = SEQS // group
    stacked_in = inputs.astype(jnp.float32).reshape(count, group, LEN, D)
    stacked_ids = block_ids.reshape(count, group, LEN)
    stacked_grad = out_grad.astype(jnp.float32).reshape(count, group, LEN, D)

    def one_group(totals, item):
        group_in, group_ids, group_grad = item

        def apply_layer(param_set, rows_in):
            return forward(param_set, rows_in, group_ids)
        result, pullback = jax.vjp(apply_layer, params, group_in)
        grad_params, grad_rows = pullback(group_grad)
        return (jax.tree.map(jnp.add, totals, grad_params), (result.astype(jnp.bfloat16), grad_rows))
    start = tuple((jnp.zeros_like(value) for value in params))
    totals, (results, grads) = lax.scan(one_group, start, (stacked_in, stacked_ids, stacked_grad))
    grad_gain_one, grad_shift_one, grad_proj, grad_qbias, grad_vbias, grad_out, grad_obias, grad_gain_two, grad_shift_two, grad_exp, grad_ebias, grad_red, grad_rbias = totals
    return (results.reshape(SEQS, LEN, D), grads.reshape(SEQS, LEN, D), grad_gain_one, grad_shift_one, grad_proj, grad_qbias, grad_vbias, grad_out, grad_obias, grad_gain_two, grad_shift_two, grad_exp, grad_ebias, grad_red, grad_rbias)
```

```python
import functools
import math

import jax
import jax.numpy as jnp
from jax import lax
from jax.experimental import pallas as pl
from jax.experimental.pallas import tpu as pltpu
from jax.sharding import Mesh, PartitionSpec as P

H = 12
HD = 64
EPSILON = 1e-05
GELU_C = 0.7978845608028654
GELU_A = 0.044715
MASKED = -1e30
SCALE = 1.0 / math.sqrt(HD)
PARTS = 4
TILE = 256
f32 = jnp.float32
bf16 = jnp.bfloat16
VM = pl.BlockSpec(memory_space=pltpu.VMEM)
SM = pl.BlockSpec(memory_space=pltpu.SMEM)


def dot(left, right, left_dim, right_dim):
    return lax.dot_general(
        left, right, (((left_dim,), (right_dim,)), ((), ())), preferred_element_type=f32
    )


def kernel_call(body, outs, args, scratch=(), flops=0, moved=0, name=None):
    return pl.pallas_call(
        body,
        out_shape=[jax.ShapeDtypeStruct(s, d) for s, d in outs],
        in_specs=[SM] + [VM] * (len(args) - 1),
        out_specs=[VM] * len(outs),
        scratch_shapes=[pltpu.VMEM(s, d) for s, d in scratch],
        compiler_params=pltpu.CompilerParams(vmem_limit_bytes=58 * 2**20),
        cost_estimate=pl.CostEstimate(flops=flops, bytes_accessed=moved, transcendentals=0),
        name=name,
    )(*args)


def normalize(rows):
    average = jnp.mean(rows, axis=-1, keepdims=True)
    centered = rows - average
    variance = jnp.mean(centered * centered, axis=-1, keepdims=True)
    inv_std = lax.rsqrt(variance + EPSILON)
    return centered * inv_std, inv_std


def norm_backward(grad_rows, normed, inv_std, gain):
    scaled = grad_rows * gain
    first_mean = jnp.mean(scaled, axis=-1, keepdims=True)
    second_mean = jnp.mean(scaled * normed, axis=-1, keepdims=True)
    return inv_std * (scaled - first_mean - normed * second_mean)


def gelu_parts(pre):
    square = pre * pre
    tangent = jnp.tanh(GELU_C * (pre + GELU_A * pre * square))
    half = 0.5 * (1.0 + tangent)
    value = pre * half
    slope = half + 0.5 * pre * (1.0 - tangent * tangent) * GELU_C * (1.0 + 3.0 * GELU_A * square)
    return value, slope


def offset(index, step):
    return pl.multiple_of(index * step, step)


def mask_features(ids, rows):
    lane = lax.broadcasted_iota(jnp.int32, (rows, HD), 1).astype(f32)
    own = jnp.broadcast_to(ids, (rows, HD))
    key_side = jnp.where(lane == own, 1.0, 0.0).astype(bf16)
    query_side = jnp.where((lane > own) & (lane < 4.0), MASKED, 0.0).astype(bf16)
    return query_side, key_side


def attend_kernel(
    tab, x_own, x_oth, ids, w_own, w_one, w_two, gain, shift, bias,
    att, proj, lse, normed, w_nat, qa, ka, va, mixed, lcol,
):
    half = x_own.shape[0]
    rows = 2 * half
    piece = w_own.shape[0]
    group = att.shape[1]
    per_dev = group // HD
    core = tab[0]
    w_nat[pl.ds(offset(tab[1], piece), piece), :] = w_own[...]
    w_nat[pl.ds(offset(tab[2], piece), piece), :] = w_two[0]
    w_nat[pl.ds(offset(tab[3], piece), piece), :] = w_one[...]
    w_nat[pl.ds(offset(tab[4], piece), piece), :] = w_two[1]
    for ref, place in ((x_own, core), (x_oth, 1 - core)):
        full, _ = normalize(ref[...].astype(f32))
        normed[pl.ds(offset(place, half), half), :] = (full * gain[...] + shift[...]).astype(bf16)
    query_side, key_side = mask_features(ids[...], rows)
    for part in range(3):
        for pair in range(per_dev // 2):
            col = part * group + pair * 2 * HD
            low = (dot(normed[...], w_nat[:, col : col + 2 * HD], 1, 0) + bias[:, col : col + 2 * HD]).astype(bf16)
            proj[:, col : col + 2 * HD] = low
            for side in range(2):
                one = low[:, side * HD : (side + 1) * HD]
                head = 2 * pair + side
                if part == 0:
                    qa[head] = jnp.concatenate([one * jnp.asarray(SCALE, bf16), query_side], axis=1)
                elif part == 1:
                    ka[head] = jnp.concatenate([one, key_side], axis=1)
                else:
                    va[head] = one
    lane = lax.broadcasted_iota(jnp.int32, (TILE, 128), 1)

    def one_head(head, carry):
        for tile in range(rows // TILE):
            span = slice(tile * TILE, (tile + 1) * TILE)
            scores = dot(qa[head, span, :], ka[head], 1, 1)
            peak = jnp.max(scores, axis=1, keepdims=True)
            raised = jnp.exp(scores - peak)
            summed = jnp.sum(raised, axis=1, keepdims=True)
            out = dot(raised.astype(bf16), va[head], 1, 0) / summed
            mixed[head, span, :] = out.astype(bf16)
            lcol[span, :] = jnp.where(
                lane == head, jnp.broadcast_to(peak + jnp.log(summed), (TILE, 128)), lcol[span, :]
            )
        return carry

    lcol[...] = jnp.zeros_like(lcol)
    lax.fori_loop(0, per_dev, one_head, 0)
    for pair in range(per_dev // 2):
        att[:, pair * 2 * HD : (pair + 1) * 2 * HD] = jnp.concatenate(
            [mixed[2 * pair], mixed[2 * pair + 1]], axis=1
        )
    lse[...] = jnp.transpose(lcol[...])[:8, :]


def mix_kernel(tab, x_own, att_own, att_oth, w_own, w_one, w_two, obias, gain, shift, middle, normed, w_nat):
    half, width = x_own.shape
    piece = w_own.shape[0]
    group = att_own.shape[1]
    core = tab[0]
    w_nat[pl.ds(offset(tab[1], piece), piece), :] = w_own[:, :width]
    w_nat[pl.ds(offset(tab[2], piece), piece), :] = w_two[0, :, :width]
    w_nat[pl.ds(offset(tab[3], piece), piece), :] = w_one[:, :width]
    w_nat[pl.ds(offset(tab[4], piece), piece), :] = w_two[1, :, :width]
    span = pl.ds(offset(core, half), half)
    total = x_own[...].astype(f32) + (
        dot(att_own[span, :], w_nat[pl.ds(offset(core, group), group), :], 1, 0)
        + dot(att_oth[span, :], w_nat[pl.ds(offset(1 - core, group), group), :], 1, 0)
        + obias[...]
    )
    middle[...] = total
    full, _ = normalize(total)
    normed[...] = (full * gain[...] + shift[...]).astype(bf16)


def feed_kernel(
    tab, nm_own, nm_oth, g_own, g_oth, e_own, e_one, e_two, r_own, r_one, r_two, ebias,
    out_own, out_oth, dy_own, dy_oth, red_keep, red_send, exp_keep, exp_send, bias_sum,
    nm, gt, we, out_acc, dy_acc,
):
    half, width = nm_own.shape
    piece = e_own.shape[0]
    block = r_own.shape[0]
    hidden = PARTS * block
    nm[:half, :] = nm_own[...]
    nm[half:, :] = nm_oth[...]
    gt[:half, :] = g_own[...]
    gt[half:, :] = g_oth[...]
    cols = slice(width, width + hidden)
    we[pl.ds(offset(tab[1], piece), piece), :] = e_own[:, cols]
    we[pl.ds(offset(tab[2], piece), piece), :] = e_two[0, :, cols]
    we[pl.ds(offset(tab[3], piece), piece), :] = e_one[:, cols]
    we[pl.ds(offset(tab[4], piece), piece), :] = e_two[1, :, cols]
    for rel in range(PARTS):
        place = pl.ds(offset(tab[1 + rel], block), block)
        w_red = (r_own[...], r_two[0], r_one[...], r_two[1])[rel]
        w_exp = we[:, place]
        pre = dot(nm[...], w_exp, 1, 0) + ebias[:, place]
        value, slope = gelu_parts(pre)
        active = value.astype(bf16)
        part_out = dot(active, w_red, 1, 0)
        grad_red = dot(active, gt[...], 0, 0).astype(bf16)
        if rel < 2:
            red_keep[rel] = grad_red
        else:
            red_send[rel - 2] = grad_red
        grad_hidden32 = dot(gt[...], w_red, 1, 1) * slope
        grad_hidden = grad_hidden32.astype(bf16)
        bias_sum[:, place] = jnp.sum(grad_hidden.astype(f32), axis=0, keepdims=True)
        grad_exp = dot(nm[...], grad_hidden, 0, 0).astype(bf16)
        for chip in range(PARTS):
            rows = grad_exp[chip * piece : (chip + 1) * piece, :]
            for target in range(PARTS):

                @pl.when(tab[1 + target] == chip)
                def _():
                    if target < 2:
                        exp_keep[target, :, place] = rows
                    else:
                        exp_send[target - 2, :, place] = rows

        part_dy = dot(grad_hidden, w_exp, 1, 1)
        if rel == 0:
            out_acc[...] = part_out
            dy_acc[...] = part_dy
        else:
            out_acc[...] += part_out
            dy_acc[...] += part_dy
    out_own[...] = out_acc[:half, :]
    out_oth[...] = out_acc[half:, :].astype(bf16)
    dy_own[...] = dy_acc[:half, :]
    dy_oth[...] = dy_acc[half:, :].astype(bf16)


def second_kernel(
    tab, middle, dy_own, dy_in, g_own, out_own, out_in, gain, rbias,
    grad_middle, branch, result, sums,
):
    grad_rows = dy_own[...] + dy_in[...].astype(f32)
    mid = middle[...]
    full, inv_std = normalize(mid)
    top = g_own[...].astype(f32)
    total = top + norm_backward(grad_rows, full, inv_std, gain[...])
    low = total.astype(bf16)
    grad_middle[...] = total
    branch[...] = low
    result[...] = (mid + (out_own[...] + out_in[...].astype(f32) + rbias[...])).astype(bf16)
    sums[0:1, :] = jnp.sum(grad_rows * full, axis=0, keepdims=True)
    sums[1:2, :] = jnp.sum(grad_rows, axis=0, keepdims=True)
    sums[2:3, :] = jnp.sum(low.astype(f32), axis=0, keepdims=True)
    sums[3:4, :] = jnp.sum(top, axis=0, keepdims=True)
    sums[4:8, :] = jnp.zeros((4, mid.shape[1]), f32)


def attend_back_kernel(
    tab, gb_own, gb_oth, w_nat, proj, lse, ids, att_own, att_oth,
    dproj, out_keep, out_send, sums, gb, qa, ka, va, kt, do, dq, dk, dv,
):
    half, width = gb_own.shape
    rows = 2 * half
    group = att_own.shape[1]
    per_dev = group // HD
    piece = out_keep.shape[1]
    core = tab[0]
    gb[pl.ds(offset(core, half), half), :] = gb_own[...]
    gb[pl.ds(offset(1 - core, half), half), :] = gb_oth[...]
    query_side, key_side = mask_features(ids[...], rows)
    for pair in range(per_dev // 2):
        cols = [part * group + pair * 2 * HD for part in range(3)]
        query, keys, values = [proj[:, c : c + 2 * HD] for c in cols]
        w_rows = w_nat[pl.ds(pl.multiple_of(core * group + pair * 2 * HD, 2 * HD), 2 * HD), :]
        grad_att = dot(gb[...], w_rows, 1, 1).astype(bf16)
        keys_t = jnp.transpose(keys)
        for side in range(2):
            head = 2 * pair + side
            span = slice(side * HD, (side + 1) * HD)
            qa[head] = jnp.concatenate([query[:, span] * jnp.asarray(SCALE, bf16), query_side], axis=1)
            ka[head] = jnp.concatenate([keys[:, span], key_side], axis=1)
            va[head] = values[:, span]
            kt[head] = keys_t[span, :]
            do[head] = grad_att[:, span]

    def one_head(head, carry):
        for tile in range(rows // TILE):
            span = slice(tile * TILE, (tile + 1) * TILE)
            query = qa[head, span, :]
            grad_mix = do[head, span, :]
            scores = dot(ka[head], query, 1, 1)
            prob = jnp.exp(scores - lse[pl.ds(head, 1), span])
            grad_prob = dot(va[head], grad_mix, 1, 1)
            centre = jnp.sum(prob * grad_prob, axis=0, keepdims=True)
            grad_scores = (prob * (grad_prob - centre)).astype(bf16)
            part_v = dot(prob.astype(bf16), grad_mix, 1, 0)
            part_k = dot(grad_scores, query, 1, 0)[:, :HD]
            part_q = dot(kt[head], grad_scores, 1, 0) * SCALE
            dq[head, span, :] = jnp.transpose(part_q)
            if tile == 0:
                dv[head] = part_v
                dk[head] = part_k
            else:
                dv[head] += part_v
                dk[head] += part_k
        return carry

    lax.fori_loop(0, per_dev, one_head, 0)
    for part, ref in enumerate((dq, dk, dv)):
        for pair in range(per_dev // 2):
            col = part * group + pair * 2 * HD
            low = jnp.concatenate([ref[2 * pair], ref[2 * pair + 1]], axis=1).astype(bf16)
            dproj[:, col : col + 2 * HD] = low
            sums[:, col : col + 2 * HD] = jnp.broadcast_to(
                jnp.sum(low.astype(f32), axis=0, keepdims=True), (8, 2 * HD)
            )
    gb_cols = gb[:, pl.ds(offset(core, group), group)]
    first = dot(att_own[...], gb_cols, 0, 0).astype(bf16)
    second = dot(att_oth[...], gb_cols, 0, 0).astype(bf16)
    per_core = PARTS // 2
    for side in range(2):
        for local in range(per_core):
            lo = first[local * piece : (local + 1) * piece, :]
            hi = second[local * piece : (local + 1) * piece, :]
            chip = side * per_core + local
            rows_out = jnp.where(core == side, lo, hi)
            for target in range(PARTS):

                @pl.when(tab[1 + target] == chip)
                def _():
                    if target < 2:
                        out_keep[target] = rows_out
                    else:
                        out_send[target - 2] = rows_out


def project_back_kernel(tab, normed, dproj, w_nat, keep, send, dy_own, dy_oth):
    half = dy_own.shape[0]
    piece = keep.shape[1]
    core = tab[0]
    own = pl.ds(offset(core, half), half)
    oth = pl.ds(offset(1 - core, half), half)
    dy_oth[...] = dot(dproj[oth, :], w_nat[...], 1, 1).astype(bf16)
    dy_own[...] = dot(dproj[own, :], w_nat[...], 1, 1)
    grad = dot(normed[...], dproj[...], 0, 0).astype(bf16)
    for chip in range(PARTS):
        rows = grad[chip * piece : (chip + 1) * piece, :]
        for target in range(PARTS):

            @pl.when(tab[1 + target] == chip)
            def _():
                if target < 2:
                    keep[target] = rows
                else:
                    send[target - 2] = rows


def first_kernel(tab, x_own, dy_own, dy_in, grad_middle, gain, out, sums):
    grad_rows = dy_own[...] + dy_in[...].astype(f32)
    full, inv_std = normalize(x_own[...].astype(f32))
    total = grad_middle[...] + norm_backward(grad_rows, full, inv_std, gain[...])
    out[...] = total.astype(bf16)
    sums[0:1, :] = jnp.sum(grad_rows * full, axis=0, keepdims=True)
    sums[1:2, :] = jnp.sum(grad_rows, axis=0, keepdims=True)
    sums[2:8, :] = jnp.zeros((6, full.shape[1]), f32)


def per_device(
    inputs, block_ids, first_gain, first_shift, w_project, query_bias, value_bias, w_output,
    output_bias, second_gain, second_shift, w_expand, expand_bias, w_reduce, reduce_bias, out_grad,
):
    seq_dev, local, width = inputs.shape
    chips = lax.axis_size("chip")
    groups = lax.axis_size("sp")
    half = 2 * local
    rows = 2 * half
    group = width // 2
    own_rows = w_project.shape[0]
    own_hidden = w_reduce.shape[0]
    hidden = chips * own_hidden
    piece = width // PARTS
    block = hidden // PARTS
    core = lax.axis_index("core")
    chip = lax.axis_index("chip")
    zed = lax.axis_index("sp")
    parity = lax.rem(zed, 2)
    grid_like = chips == PARTS

    swap_pairs = [(0, 1), (1, 0)]

    def swap(value):
        return lax.ppermute(value, "core", swap_pairs)

    def seq_pairs(turn):
        return [
            (c * groups + z, (z // 2) * groups + 2 * c + (z + turn) % 2)
            for c in range(2)
            for z in range(groups)
        ]

    def to_sequence(payload):
        low, high = payload
        got = [
            lax.ppermute(jnp.where(lax.rem(zed + turn, 2) == 0, low, high), ("core", "sp"), seq_pairs(turn))
            for turn in range(2)
        ]
        return jnp.where(parity == 0, got[0], got[1]), jnp.where(parity == 0, got[1], got[0])

    def from_sequence(low, high):
        got = []
        for turn in range(2):
            pairs = [(b, a) for a, b in seq_pairs(turn)]
            got.append(
                lax.ppermute(jnp.where(lax.rem(zed + turn, 2) == 0, low, high), ("core", "sp"), pairs)
            )
        return jnp.stack(
            [jnp.where(parity == 0, got[0], got[1]), jnp.where(parity == 0, got[1], got[0])]
        )

    def plane_pairs(step):
        pairs = []
        for i in range(PARTS):
            for c in range(2):
                flip = (1, 2)[c] if step == 0 else (2, 1)[c]
                pairs.append((i * 2 + c, (i ^ flip) * 2 + c))
        return pairs

    def plane(value, step):
        return lax.ppermute(value, ("chip", "core"), plane_pairs(step))

    if grid_like:
        flips = jnp.where(core == 0, jnp.array([0, 2, 1, 3]), jnp.array([0, 1, 2, 3]))
        order = (chip ^ flips).astype(jnp.int32)
    else:
        order = jnp.arange(PARTS, dtype=jnp.int32)
    tab = jnp.concatenate([core[None].astype(jnp.int32), order])

    def gather(value):
        if grid_like:
            one = plane(value, 0)
            two = plane(jnp.stack([value, one]), 1)
            return value, one, two
        full = lax.all_gather(value, "chip", axis=0, tiled=True)
        full = full.reshape(PARTS, full.shape[0] // PARTS, full.shape[1])
        return full[0], full[2], jnp.stack([full[1], full[3]])

    def reduce_plane(keep, send):
        if grid_like:
            total = (keep.astype(f32) + plane(send, 0).astype(f32)).astype(bf16)
            return (total[0].astype(f32) + plane(total[1], 1).astype(f32)).astype(bf16)
        full = jnp.concatenate([keep, send]).reshape(-1, keep.shape[2])
        return lax.psum_scatter(full, "chip", scatter_dimension=0, tiled=True)

    def reduce_line(value):
        for flip in (1, 2):
            pairs = [(z, z ^ flip) for z in range(groups)]
            value = (value.astype(f32) + lax.ppermute(value, "sp", pairs).astype(f32)).astype(bf16)
        return value

    id_rows = jnp.pad(block_ids.astype(bf16)[:, None, :], ((0, 0), (0, 15), (0, width - local)))
    packed = jnp.concatenate([inputs, id_rows], axis=1)

    def halves(target):
        wp = lax.dynamic_index_in_dim(w_project.reshape(own_rows, 3, 2, group), target, 2, False)
        we = lax.dynamic_index_in_dim(
            w_expand.reshape(own_rows, chips, 2, own_hidden), target, 2, False
        )
        return wp.reshape(own_rows, 3 * group), we.reshape(own_rows, hidden)

    small = jnp.concatenate(
        [first_gain, first_shift, query_bias, value_bias, output_bias, second_gain, second_shift,
         reduce_bias, expand_bias]
    )
    small_row = jnp.pad(small[None, :], ((0, 15), (0, 3 * group - small.shape[0])))
    wp_mine, we_mine = halves(core)
    wp_part, we_part = halves(1 - core)
    mine_a = jnp.concatenate([wp_mine, small_row])
    mine_b = jnp.concatenate([w_output, we_mine], axis=1)
    got_a = swap(jnp.concatenate([wp_part, small_row]))
    got_b = swap(jnp.concatenate([w_output, we_part], axis=1))

    def ordered(mine, other):
        return jnp.where(core == 0, jnp.stack([mine, other]), jnp.stack([other, mine]))

    block_a = ordered(mine_a, got_a)
    wp_block = block_a[:, :own_rows].reshape(2 * own_rows, 3 * group)
    small_block = block_a[:, own_rows]
    wo_block = ordered(mine_b, got_b).reshape(2 * own_rows, width + hidden)

    low_x, high_x = to_sequence(packed)
    if grid_like:
        first_block = jnp.concatenate([wp_block, jnp.pad(small_block, ((0, 14), (0, 0)))])
        a_own, a_one, a_two = gather(first_block)
        picked = [a_own[2 * own_rows :][:2], a_two[0, 2 * own_rows :][:2], a_one[2 * own_rows :][:2],
                  a_two[1, 2 * own_rows :][:2]]
        rows_of = []
        for target in range(PARTS):
            value = picked[0]
            for rel in range(1, PARTS):
                value = jnp.where(order[rel] == target, picked[rel], value)
            rows_of.append(value)
        small_all = jnp.concatenate(rows_of)
        a_pieces = (a_own[:piece], a_one[:piece], a_two[:, :piece])
    else:
        a_pieces = gather(wp_block)
        small_all = lax.all_gather(small_block, "chip", axis=0, tiled=True)
    small_all = small_all.astype(f32)

    def vector(index):
        return small_all[:, index * own_rows : (index + 1) * own_rows].reshape(1, width)

    gain_one, shift_one, qbias, vbias, obias, gain_two, shift_two, rbias = [vector(i) for i in range(8)]
    ebias = lax.dynamic_index_in_dim(
        small_all[:, 8 * own_rows : 8 * own_rows + own_hidden].reshape(chips, 2, own_hidden), core, 1, False
    ).reshape(1, hidden)
    qbias_own = lax.dynamic_slice_in_dim(qbias, core * group, group, 1)
    vbias_own = lax.dynamic_slice_in_dim(vbias, core * group, group, 1)
    bias_all = jnp.concatenate([qbias_own, jnp.zeros_like(qbias_own), vbias_own], axis=1)

    own_packed = jnp.stack([low_x, high_x])
    oth_packed = swap(own_packed)
    x_own = own_packed[:, :local].reshape(half, width)
    x_oth = oth_packed[:, :local].reshape(half, width)
    ids_own = own_packed[:, local, :local].reshape(half)
    ids_oth = oth_packed[:, local, :local].reshape(half)
    ids = jnp.where(
        core == 0, jnp.concatenate([ids_own, ids_oth]), jnp.concatenate([ids_oth, ids_own])
    ).astype(f32)[:, None]

    b_pieces = gather(wo_block)
    r_pieces = gather(w_reduce)
    g_own = jnp.concatenate(to_sequence(out_grad))
    g_oth = swap(g_own)

    per_dev = group // HD
    att, proj, lse, normed_in, wp_nat = kernel_call(
        attend_kernel,
        [((rows, group), bf16), ((rows, 3 * group), bf16), ((8, rows), f32), ((rows, width), bf16),
         ((width, 3 * group), bf16)],
        (tab, x_own, x_oth, ids, *a_pieces, gain_one, shift_one, bias_all),
        [((per_dev, rows, 2 * HD), bf16), ((per_dev, rows, 2 * HD), bf16), ((per_dev, rows, HD), bf16),
         ((per_dev, rows, HD), bf16), ((rows, 128), f32)],
        flops=2 * rows * width * 3 * group + per_dev * rows * rows * HD * 16,
        moved=2**23,
        name="attend",
    )
    att_oth = swap(att)
    middle, nm_own, wo_nat = kernel_call(
        mix_kernel,
        [((half, width), f32), ((half, width), bf16), ((width, width), bf16)],
        (tab, x_own, att, att_oth, *b_pieces, obias, gain_two, shift_two),
        flops=2 * half * width * width,
        moved=2**23,
        name="mix",
    )
    nm_oth = swap(nm_own)
    (out_own, out_oth, dy_own, dy_oth, red_keep, red_send, exp_keep, exp_send, ebias_sum) = kernel_call(
        feed_kernel,
        [((half, width), f32), ((half, width), bf16), ((half, width), f32), ((half, width), bf16),
         ((2, block, width), bf16), ((2, block, width), bf16), ((2, piece, hidden), bf16),
         ((2, piece, hidden), bf16), ((1, hidden), f32)],
        (tab, nm_own, nm_oth, g_own, g_oth, *b_pieces, *r_pieces, ebias),
        [((rows, width), bf16), ((rows, width), bf16), ((width, hidden), bf16), ((rows, width), f32),
         ((rows, width), f32)],
        flops=12 * rows * width * hidden,
        moved=2**24,
        name="feed",
    )
    dy_in = swap(dy_oth)
    out_in = swap(out_oth)
    red_part = reduce_plane(red_keep, red_send)
    exp_part = reduce_plane(exp_keep, exp_send)
    grad_middle, gb_own, result, sums_two = kernel_call(
        second_kernel,
        [((half, width), f32), ((half, width), bf16), ((half, width), bf16), ((8, width), f32)],
        (tab, middle, dy_own, dy_in, g_own, out_own, out_in, gain_two, rbias),
        flops=half * width * 30,
        moved=2**23,
        name="second",
    )
    gb_oth = swap(gb_own)
    layer_output = from_sequence(result[:local], result[local:])
    dproj, out_keep, out_send, proj_sums = kernel_call(
        attend_back_kernel,
        [((rows, 3 * group), bf16), ((2, piece, group), bf16), ((2, piece, group), bf16), ((8, 3 * group), f32)],
        (tab, gb_own, gb_oth, wo_nat, proj, lse, ids, att, att_oth),
        [((rows, width), bf16), ((per_dev, rows, 2 * HD), bf16), ((per_dev, rows, 2 * HD), bf16),
         ((per_dev, rows, HD), bf16), ((per_dev, HD, rows), bf16), ((per_dev, rows, HD), bf16),
         ((per_dev, rows, HD), f32), ((per_dev, rows, HD), f32), ((per_dev, rows, HD), f32)],
        flops=per_dev * rows * rows * HD * 40,
        moved=2**23,
        name="attend_back",
    )
    red_all = reduce_line(red_part)
    exp_all = reduce_line(exp_part)
    proj_keep, proj_send, dx_own, dx_oth = kernel_call(
        project_back_kernel,
        [((2, piece, 3 * group), bf16), ((2, piece, 3 * group), bf16), ((half, width), f32), ((half, width), bf16)],
        (tab, normed_in, dproj, wp_nat),
        flops=4 * rows * width * 3 * group,
        moved=2**23,
        name="project_back",
    )
    dx_in = swap(dx_oth)
    grad_in, sums_one = kernel_call(
        first_kernel,
        [((half, width), bf16), ((8, width), f32)],
        (tab, x_own, dx_own, dx_in, grad_middle, gain_one),
        flops=half * width * 30,
        moved=2**22,
        name="first",
    )
    input_grad = from_sequence(grad_in[:local], grad_in[local:]).astype(f32)

    def spread(value):
        return jnp.where(
            core == 0,
            jnp.concatenate([value, jnp.zeros_like(value)]),
            jnp.concatenate([jnp.zeros_like(value), value]),
        )

    vectors = [sums_one[0], sums_one[1], spread(proj_sums[0, :group]), spread(proj_sums[0, 2 * group :]),
               sums_two[2], sums_two[0], sums_two[1], sums_two[3]]
    owners = 2 * chips
    table = jnp.concatenate([v.reshape(owners, own_rows) for v in vectors], axis=1)
    eb = ebias_sum.reshape(chips, 1, own_hidden)
    eb_rows = jnp.where(jnp.arange(2)[None, :, None] == core, eb, 0.0).reshape(owners, own_hidden)
    table = jnp.concatenate([table, eb_rows], axis=1)
    pay = width + group + group
    table = jnp.pad(table, ((0, 0), (0, pay - table.shape[1]))).astype(bf16)
    both_keep = jnp.concatenate([out_keep, proj_keep], axis=2)
    both_send = jnp.concatenate([out_send, proj_send], axis=2)
    if grid_like:
        table = table.reshape(PARTS, 2, pay)
        table = jnp.pad(table, ((0, 0), (0, 14), (0, 0)))
        picked = []
        for rel in range(PARTS):
            value = table[0]
            for target in range(1, PARTS):
                value = jnp.where(order[rel] == target, table[target], value)
            picked.append(value)
        both_keep = jnp.concatenate([both_keep, jnp.stack(picked[:2])], axis=1)
        both_send = jnp.concatenate([both_send, jnp.stack(picked[2:])], axis=1)
        last = reduce_line(reduce_plane(both_keep, both_send))
        last_rows, last_small = last[: 2 * own_rows], last[2 * own_rows : 2 * own_rows + 2]
    else:
        last_rows = reduce_line(reduce_plane(both_keep, both_send))
        last_small = reduce_line(lax.psum_scatter(table, "chip", scatter_dimension=0, tiled=True))

    def mine_of(value, target):
        return lax.dynamic_slice_in_dim(value, target * own_rows, own_rows, 0)

    exp_mine, exp_got = mine_of(exp_all, core), swap(mine_of(exp_all, 1 - core))
    sent = jnp.concatenate([
        mine_of(last_rows, 1 - core),
        jnp.pad(lax.dynamic_slice_in_dim(last_small, 1 - core, 1, 0), ((0, 15), (0, 0))),
    ])
    got = swap(sent)
    last_mine, last_got = mine_of(last_rows, core), got[:own_rows]
    small_sum = lax.dynamic_slice_in_dim(last_small, core, 1, 0)[0].astype(f32) + got[own_rows].astype(f32)

    def woven(mine, other, parts):
        shape = (own_rows, parts, mine.shape[1] // parts)
        mine, other = mine.reshape(shape), other.reshape(shape)
        both = jnp.where(core == 0, jnp.stack([mine, other], axis=2), jnp.stack([other, mine], axis=2))
        return both.reshape(own_rows, -1).astype(f32)

    grad_expand = woven(exp_mine, exp_got, chips)
    grad_output = woven(last_mine[:, :group], last_got[:, :group], 1)
    grad_project = woven(last_mine[:, group:], last_got[:, group:], 3)
    cut = [small_sum[i * own_rows : (i + 1) * own_rows] for i in range(8)]
    return (
        layer_output,
        input_grad,
        cut[0],
        cut[1],
        grad_project,
        cut[2],
        cut[3],
        grad_output,
        cut[4],
        cut[5],
        cut[6],
        grad_expand,
        small_sum[8 * own_rows : 8 * own_rows + own_hidden],
        red_all.astype(f32),
        cut[7],
    )


def solution(mesh):
    owners, groups = mesh.shape["fsdp"], mesh.shape["sp"]
    split = Mesh(mesh.devices.reshape(owners // 2, 2, groups), ("chip", "core", "sp"))
    own = ("chip", "core")
    rows, flat, both = P(own, None), P(own), P(own, "sp", None)
    return jax.shard_map(
        per_device,
        mesh=split,
        in_specs=(both, P(own, "sp"), flat, flat, rows, flat, flat, rows, flat, flat, flat, rows, flat,
                  rows, flat, both),
        out_specs=(both, both, flat, flat, rows, flat, flat, rows, flat, flat, flat, rows, flat, rows, flat),
        check_vma=False,
    )
```

```python
import functools
import math

import jax
import jax.numpy as jnp
from jax import lax
from jax.experimental import pallas as pl
from jax.experimental.pallas import tpu as pltpu
from jax.sharding import Mesh, PartitionSpec as P

H = 12
HD = 64
EPSILON = 1e-05
GELU_C = 0.7978845608028654
GELU_A = 0.044715
MASKED = -1e30
SCALE = 1.0 / math.sqrt(HD)
PARTS = 4
TILE = 256
f32 = jnp.float32
bf16 = jnp.bfloat16
VM = pl.BlockSpec(memory_space=pltpu.VMEM)
SM = pl.BlockSpec(memory_space=pltpu.SMEM)


def dot(left, right, left_dim, right_dim):
    return lax.dot_general(
        left, right, (((left_dim,), (right_dim,)), ((), ())), preferred_element_type=f32
    )


def kernel_call(body, outs, args, scratch=(), flops=0, moved=0, name=None):
    return pl.pallas_call(
        body,
        out_shape=[jax.ShapeDtypeStruct(s, d) for s, d in outs],
        in_specs=[SM] + [VM] * (len(args) - 1),
        out_specs=[VM] * len(outs),
        scratch_shapes=[pltpu.VMEM(s, d) for s, d in scratch],
        compiler_params=pltpu.CompilerParams(vmem_limit_bytes=58 * 2**20),
        cost_estimate=pl.CostEstimate(flops=flops, bytes_accessed=moved, transcendentals=0),
        name=name,
    )(*args)


def normalize(rows):
    average = jnp.mean(rows, axis=-1, keepdims=True)
    centered = rows - average
    variance = jnp.mean(centered * centered, axis=-1, keepdims=True)
    inv_std = lax.rsqrt(variance + EPSILON)
    return centered * inv_std, inv_std


def norm_backward(grad_rows, normed, inv_std, gain):
    scaled = grad_rows * gain
    first_mean = jnp.mean(scaled, axis=-1, keepdims=True)
    second_mean = jnp.mean(scaled * normed, axis=-1, keepdims=True)
    return inv_std * (scaled - first_mean - normed * second_mean)


def gelu_parts(pre):
    square = pre * pre
    tangent = jnp.tanh(GELU_C * (pre + GELU_A * pre * square))
    half = 0.5 * (1.0 + tangent)
    value = pre * half
    slope = half + 0.5 * pre * (1.0 - tangent * tangent) * GELU_C * (1.0 + 3.0 * GELU_A * square)
    return value, slope


def offset(index, step):
    return pl.multiple_of(index * step, step)


def prep_kernel(tab, x, ids, wp, wo, we, small, send0, send1, a_mine, a_part, b_mine, b_part):
    local, width = x.shape[1:]
    rows = wp.shape[0]
    core, par = tab[0], tab[5]
    group = width // 2
    lane = lax.broadcasted_iota(jnp.int32, (16, local), 0)
    for turn, out in enumerate((send0, send1)):
        which = lax.rem(par + turn, 2)
        out[:local, :] = x[which]
        line = jnp.where(which == 0, ids[0:1, :], ids[1:2, :])
        out[local:, :] = jnp.zeros((16, width), bf16)
        out[local:, :local] = jnp.broadcast_to(line, (16, local)).astype(bf16)
    for out, place in ((a_mine, core), (a_part, 1 - core)):
        for part in range(3):
            out[:rows, part * group : (part + 1) * group] = wp[
                :, pl.ds(pl.multiple_of(part * width + place * group, group), group)
            ]
        out[rows:, :] = small[...]
    for out, place in ((b_mine, core), (b_part, 1 - core)):
        out[:, :width] = wo[...]
        block = we.shape[1] // (2 * PARTS)
        for chip in range(PARTS):
            out[:, width + chip * block : width + (chip + 1) * block] = we[
                :, pl.ds(pl.multiple_of((2 * chip + place) * block, block), block)
            ]


def fill(target, pieces, tab, cols, piece):
    own, one, two, far = pieces
    step = own.shape[0] // 2
    seg = piece // 2
    for rel, ref in enumerate((own, two, one, far)):
        for side in range(2):
            target[pl.ds(pl.multiple_of(tab[1 + rel] * piece + side * seg, seg), seg), :] = ref[
                side * step : side * step + seg, cols
            ]


def natural(tab, place, turn, local):
    return pl.ds(pl.multiple_of(place * 2 * local + lax.rem(tab[5] + turn, 2) * local, local), local)


def attend_kernel(
    tab, p0, p1, q0, q1, w_own, w_one, w_two, w_far, vec,
    att, qkv0, qkv1, qkv2, lse, normed_t, wp0, wp1, wp2, masks, w_nat, normed, qa, ka, va, mixed, lcol,
):
    local = p0.shape[0] - 16
    rows = 4 * local
    width = normed.shape[1]
    group = att.shape[1]
    per_dev = group // HD
    core = tab[0]
    fill(w_nat, (w_own, w_one, w_two, w_far), tab, slice(None), width // PARTS)
    gain, shift = vec[0:1, :], vec[1:2, :]
    lane = lax.broadcasted_iota(jnp.int32, (local, HD), 1).astype(f32)
    for place, refs in ((core, (p0, p1)), (1 - core, (q0, q1))):
        for turn, ref in enumerate(refs):
            span = natural(tab, place, turn, local)
            full, _ = normalize(ref[:local, :].astype(f32))
            normed[span, :] = (full * gain + shift).astype(bf16)
            line = jnp.broadcast_to(ref[local : local + 1, :local].astype(f32), (128, local))
            own = jnp.transpose(line)[:, :HD]
            masks[span, :] = jnp.concatenate(
                [
                    jnp.where((lane > own) & (lane < 4.0), MASKED, 0.0).astype(bf16),
                    jnp.where(lane == own, 1.0, 0.0).astype(bf16),
                ],
                axis=1,
            )
    normed_t[...] = jnp.transpose(normed[...])
    query_side, key_side = masks[:, :HD], masks[:, HD:]
    own_cols = pl.ds(offset(core, group), group)
    biases = (vec[2:3, own_cols], None, vec[3:4, own_cols])
    for pair in range(per_dev // 2):
        qkv, wp = (qkv0, qkv1, qkv2)[pair], (wp0, wp1, wp2)[pair]
        for part in range(3):
            col = part * group + pair * 2 * HD
            weights = w_nat[:, col : col + 2 * HD]
            wp[:, part * 2 * HD : (part + 1) * 2 * HD] = weights
            low = dot(normed[...], weights, 1, 0)
            if biases[part] is not None:
                low = low + biases[part][:, pair * 2 * HD : (pair + 1) * 2 * HD]
            low = low.astype(bf16)
            qkv[part] = low
            for side in range(2):
                one = low[:, side * HD : (side + 1) * HD]
                head = 2 * pair + side
                if part == 0:
                    qa[head] = jnp.concatenate([one * jnp.asarray(SCALE, bf16), query_side], axis=1)
                elif part == 1:
                    ka[head] = jnp.concatenate([one, key_side], axis=1)
                else:
                    va[head] = one
    wide = lax.broadcasted_iota(jnp.int32, (TILE, 128), 1)

    def one_head(head, carry):
        for tile in range(rows // TILE):
            span = slice(tile * TILE, (tile + 1) * TILE)
            scores = dot(qa[head, span, :], ka[head], 1, 1)
            peak = jnp.max(scores, axis=1, keepdims=True)
            raised = jnp.exp(scores - peak)
            summed = jnp.sum(raised, axis=1, keepdims=True)
            out = dot(raised.astype(bf16), va[head], 1, 0) / summed
            mixed[head, span, :] = out.astype(bf16)
            lcol[span, :] = jnp.where(
                wide == head, jnp.broadcast_to(peak + jnp.log(summed), (TILE, 128)), lcol[span, :]
            )
        return carry

    lcol[...] = jnp.zeros_like(lcol)
    lax.fori_loop(0, per_dev, one_head, 0)
    for pair in range(per_dev // 2):
        att[:, pair * 2 * HD : (pair + 1) * 2 * HD] = jnp.concatenate(
            [mixed[2 * pair], mixed[2 * pair + 1]], axis=1
        )
    lse[...] = jnp.transpose(lcol[...])[:8, :]


def mix_kernel(
    tab, p0, p1, att_own, att_oth, w_own, w_one, w_two, w_far, vec, middle, normed, wo0, wo1, wo2, w_nat
):
    local = p0.shape[0] - 16
    width = w_nat.shape[1]
    group = att_own.shape[1]
    core = tab[0]
    fill(w_nat, (w_own, w_one, w_two, w_far), tab, slice(0, width), width // PARTS)
    mine = w_nat[pl.ds(offset(core, group), group), :]
    theirs = w_nat[pl.ds(offset(1 - core, group), group), :]
    for turn, ref in enumerate((p0, p1)):
        span = natural(tab, core, turn, local)
        total = ref[:local, :].astype(f32) + (
            dot(att_own[span, :], mine, 1, 0) + dot(att_oth[span, :], theirs, 1, 0) + vec[4:5, :]
        )
        place = slice(turn * local, (turn + 1) * local)
        middle[place, :] = total
        full, _ = normalize(total)
        normed[place, :] = (full * vec[5:6, :] + vec[6:7, :]).astype(bf16)
    for pair, ref in enumerate((wo0, wo1, wo2)):
        ref[...] = mine[pair * 2 * HD : (pair + 1) * 2 * HD, :]


def scatter_rows(value, tab, piece, keep, send, cols=slice(None)):
    for chip in range(PARTS):
        rows = value[chip * piece : (chip + 1) * piece, :]
        for target in range(PARTS):

            @pl.when(tab[1 + target] == chip)
            def _():
                if target < 2:
                    keep[target, :, cols] = rows
                else:
                    send[target - 2, :, cols] = rows


def feed_kernel(
    tab, nm_own, nm_oth, g0, g1, h0, h1, e_own, e_one, e_two, e_far, r_own, r_one, r_two, r_far, ebias,
    out_own, out_oth, dy_own, dy_oth, red_keep, red_send, exp_keep, exp_send, bias_sum,
    nm, gt, we, out_acc, dy_acc,
):
    half, width = nm_own.shape
    local = half // 2
    block = r_own.shape[0]
    hidden = PARTS * block
    nm[:half, :] = nm_own[...]
    nm[half:, :] = nm_oth[...]
    for index, ref in enumerate((g0, g1, h0, h1)):
        gt[index * local : (index + 1) * local, :] = ref[...]
    fill(we, (e_own, e_one, e_two, e_far), tab, slice(width, width + hidden), width // PARTS)
    for rel in range(PARTS):
        place = pl.ds(offset(tab[1 + rel], block), block)
        w_red = (r_own, r_two, r_one, r_far)[rel][...]
        w_exp = we[:, place]
        pre = dot(nm[...], w_exp, 1, 0) + ebias[:, place]
        value, slope = gelu_parts(pre)
        active = value.astype(bf16)
        part_out = dot(active, w_red, 1, 0)
        grad_red = dot(active, gt[...], 0, 0).astype(bf16)
        if rel < 2:
            red_keep[rel] = grad_red
        else:
            red_send[rel - 2] = grad_red
        grad_hidden = (dot(gt[...], w_red, 1, 1) * slope).astype(bf16)
        bias_sum[:, place] = jnp.sum(grad_hidden.astype(f32), axis=0, keepdims=True)
        grad_exp = dot(nm[...], grad_hidden, 0, 0).astype(bf16)
        scatter_rows(grad_exp, tab, width // PARTS, exp_keep, exp_send, place)
        part_dy = dot(grad_hidden, w_exp, 1, 1)
        if rel == 0:
            out_acc[...] = part_out
            dy_acc[...] = part_dy
        else:
            out_acc[...] += part_out
            dy_acc[...] += part_dy
    out_own[...] = out_acc[:half, :]
    out_oth[...] = out_acc[half:, :].astype(bf16)
    dy_own[...] = dy_acc[:half, :]
    dy_oth[...] = dy_acc[half:, :].astype(bf16)


def second_kernel(tab, middle, dy_own, dy_in, g0, g1, vec, grad_middle, branch, sums):
    local = g0.shape[0]
    sums[...] = jnp.zeros_like(sums)
    for turn, ref in enumerate((g0, g1)):
        span = slice(turn * local, (turn + 1) * local)
        grad_rows = dy_own[span, :] + dy_in[span, :].astype(f32)
        full, inv_std = normalize(middle[span, :])
        top = ref[...].astype(f32)
        total = top + norm_backward(grad_rows, full, inv_std, vec[5:6, :])
        low = total.astype(bf16)
        grad_middle[span, :] = total
        branch[span, :] = low
        sums[0:1, :] += jnp.sum(grad_rows * full, axis=0, keepdims=True)
        sums[1:2, :] += jnp.sum(grad_rows, axis=0, keepdims=True)
        sums[2:3, :] += jnp.sum(low.astype(f32), axis=0, keepdims=True)
        sums[3:4, :] += jnp.sum(top, axis=0, keepdims=True)


def back_kernel(pair, last, extra, refs):
    tab, gb_own, gb_oth, wo_pair, qkv, lse, masks, normed_t = refs[:8]
    refs = refs[8:]
    if extra == 0:
        att_own, att_oth = refs[:2]
        refs = refs[2:]
    else:
        old_keep, old_send = (refs[0], refs[1]) if not last else (None, None)
        refs = refs if last else refs[2:]
    if last:
        others, weights, refs = refs[:pair], refs[pair : 2 * pair + 1], refs[2 * pair + 1 :]
        dproj, keep, send, sums, dx_own, dx_oth = refs[:6]
        refs = refs[6:]
    else:
        dproj, keep, send, sums = refs[:4]
        refs = refs[4:]
    gb, qa, ka, kt, do, dq, dk, dv = refs
    half, width = gb_own.shape
    local = half // 2
    rows = 2 * half
    piece = keep.shape[1]
    group = width // 2
    core = tab[0]
    for place, ref in ((core, gb_own), (1 - core, gb_oth)):
        for turn in range(2):
            gb[natural(tab, place, turn, local), :] = ref[turn * local : (turn + 1) * local, :]
    pair_w = 2 * HD
    grad_att = dot(gb[...], wo_pair[...], 1, 1).astype(bf16)
    keys_t = jnp.transpose(qkv[1])
    for side in range(2):
        span = slice(side * HD, (side + 1) * HD)
        qa[side] = jnp.concatenate([qkv[0, :, span] * jnp.asarray(SCALE, bf16), masks[:, :HD]], axis=1)
        ka[side] = jnp.concatenate([qkv[1, :, span], masks[:, HD:]], axis=1)
        kt[side] = keys_t[span, :]
        do[side] = jnp.concatenate([grad_att[:, span], qkv[2, :, span]], axis=1)

    def one_head(side, carry):
        values = do[side][:, HD:]
        for tile in range(rows // TILE):
            span = slice(tile * TILE, (tile + 1) * TILE)
            query = qa[side, span, :]
            grad_mix = do[side, span, :HD]
            scores = dot(ka[side], query, 1, 1)
            prob = jnp.exp(scores - lse[pl.ds(2 * pair + side, 1), span])
            grad_prob = dot(values, grad_mix, 1, 1)
            centre = jnp.sum(prob * grad_prob, axis=0, keepdims=True)
            grad_scores = (prob * (grad_prob - centre)).astype(bf16)
            part_v = dot(prob.astype(bf16), grad_mix, 1, 0)
            part_k = dot(grad_scores, query, 1, 0)[:, :HD]
            part_q = dot(kt[side], grad_scores, 1, 0) * SCALE
            dq[side, span, :] = jnp.transpose(part_q)
            if tile == 0:
                dv[side] = part_v
                dk[side] = part_k
            else:
                dv[side] += part_v
                dk[side] += part_k
        return carry

    lax.fori_loop(0, 2, one_head, 0)
    for part, ref in enumerate((dq, dk, dv)):
        low = jnp.concatenate([ref[0], ref[1]], axis=1).astype(bf16)
        span = slice(part * pair_w, (part + 1) * pair_w)
        dproj[:, span] = low
        sums[:, span] = jnp.broadcast_to(jnp.sum(low.astype(f32), axis=0, keepdims=True), (8, pair_w))
    grad = dot(normed_t[...], dproj[...], 1, 0).astype(bf16)
    if last:
        scatter_rows(grad, tab, piece, keep, send)
        for place, out in ((1 - core, dx_oth), (core, dx_own)):
            for turn in range(2):
                span = natural(tab, place, turn, local)
                total = dot(dproj[span, :], weights[pair][...], 1, 1)
                for other in range(pair):
                    total = total + dot(others[other][span, :], weights[other][...], 1, 1)
                out[turn * local : (turn + 1) * local, :] = total.astype(out.dtype)
    elif extra == 0:
        scatter_rows(grad, tab, piece, keep, send, slice(group, 2 * group))
        gb_cols = gb[:, pl.ds(offset(core, group), group)]
        first = dot(att_own[...], gb_cols, 0, 0).astype(bf16)
        second = dot(att_oth[...], gb_cols, 0, 0).astype(bf16)
        low_rows = jnp.where(core == 0, first, second)
        high_rows = jnp.where(core == 0, second, first)
        scatter_rows(jnp.concatenate([low_rows, high_rows], axis=0), tab, piece, keep, send, slice(0, group))
    else:
        keep[:, :, : 2 * group] = old_keep[...]
        send[:, :, : 2 * group] = old_send[...]
        scatter_rows(grad, tab, piece, keep, send, slice(2 * group, 3 * group))


def first_kernel(tab, p0, p1, dy_own, dy_in, grad_middle, vec, out0, out1, sums):
    local = out0.shape[0]
    sums[...] = jnp.zeros_like(sums)
    for turn, (ref, out) in enumerate(((p0, out0), (p1, out1))):
        span = slice(turn * local, (turn + 1) * local)
        grad_rows = dy_own[span, :] + dy_in[span, :].astype(f32)
        full, inv_std = normalize(ref[:local, :].astype(f32))
        total = grad_middle[span, :] + norm_backward(grad_rows, full, inv_std, vec[0:1, :])
        out[...] = total.astype(bf16)
        sums[0:1, :] += jnp.sum(grad_rows * full, axis=0, keepdims=True)
        sums[1:2, :] += jnp.sum(grad_rows, axis=0, keepdims=True)


def after(value, *others):
    return lax.optimization_barrier((value, *others))[0]


def per_device(
    inputs, block_ids, first_gain, first_shift, w_project, query_bias, value_bias, w_output,
    output_bias, second_gain, second_shift, w_expand, expand_bias, w_reduce, reduce_bias, out_grad,
):
    seq_dev, local, width = inputs.shape
    chips = lax.axis_size("chip")
    groups = lax.axis_size("sp")
    half = 2 * local
    rows = 2 * half
    group = width // 2
    own_rows = w_project.shape[0]
    own_hidden = w_reduce.shape[0]
    hidden = chips * own_hidden
    piece = width // PARTS
    block = hidden // PARTS
    per_dev = group // HD
    pairs_dev = per_dev // 2
    pair_w = 6 * HD
    core = lax.axis_index("core")
    chip = lax.axis_index("chip")
    zed = lax.axis_index("sp")
    parity = lax.rem(zed, 2)
    grid_like = chips == PARTS
    swap_pairs = [(0, 1), (1, 0)]

    def swap(value):
        return lax.ppermute(value, "core", swap_pairs)

    def seq_pairs(turn):
        return [
            (c * groups + z, (z // 2) * groups + 2 * c + (z + turn) % 2)
            for c in range(2)
            for z in range(groups)
        ]

    def to_sequence(pieces):
        return [lax.ppermute(pieces[turn], ("core", "sp"), seq_pairs(turn)) for turn in range(2)]

    def from_sequence(pieces):
        got = [
            lax.ppermute(pieces[turn], ("core", "sp"), [(b, a) for a, b in seq_pairs(turn)])
            for turn in range(2)
        ]
        return jnp.stack(
            [jnp.where(parity == 0, got[0], got[1]), jnp.where(parity == 0, got[1], got[0])]
        )

    def plane(value, step):
        pairs = []
        for i in range(PARTS):
            for c in range(2):
                flip = (1, 2)[c] if step == 0 else (2, 1)[c]
                pairs.append((i * 2 + c, (i ^ flip) * 2 + c))
        return lax.ppermute(value, ("chip", "core"), pairs)

    if grid_like:
        flips = jnp.where(core == 0, jnp.array([0, 2, 1, 3]), jnp.array([0, 1, 2, 3]))
        order = (chip ^ flips).astype(jnp.int32)
    else:
        order = jnp.arange(PARTS, dtype=jnp.int32)
    tab = jnp.concatenate([core[None].astype(jnp.int32), order, parity[None].astype(jnp.int32)])

    def gather(value):
        if grid_like:
            one = plane(value, 0)
            return value, one, plane(value, 1), plane(one, 1)
        full = lax.all_gather(value, "chip", axis=0, tiled=True)
        full = full.reshape(PARTS, full.shape[0] // PARTS, full.shape[1])
        return full[0], full[2], full[1], full[3]

    def added(left, right):
        return (left.astype(f32) + right.astype(f32)).astype(bf16)

    def plane_one(keep, send):
        if grid_like:
            return added(keep, plane(send, 0))
        full = jnp.concatenate([keep, send]).reshape(-1, keep.shape[2])
        return lax.psum_scatter(full, "chip", scatter_dimension=0, tiled=True)

    def plane_two(total):
        return added(total[0], plane(total[1], 1)) if grid_like else total

    near = [(z, z ^ 1) for z in range(groups)]
    apart = [(z, z ^ 2) for z in range(groups)]
    low_bit, high_bit = lax.rem(zed, 2), zed // 2

    def pick(value, index):
        return lax.dynamic_index_in_dim(value, index, 0, False)

    def line_one(value):
        cut = value.reshape(2, 2, value.shape[0] // 4, value.shape[1])
        return added(pick(cut, low_bit), lax.ppermute(pick(cut, 1 - low_bit), "sp", near))

    def line_two(value):
        return added(pick(value, high_bit), lax.ppermute(pick(value, 1 - high_bit), "sp", apart))

    def line_three(value):
        other = lax.ppermute(value, "sp", apart)
        return jnp.where(high_bit == 0, jnp.concatenate([value, other]), jnp.concatenate([other, value]))

    def line_four(value):
        other = lax.ppermute(value, "sp", near)
        return jnp.where(low_bit == 0, jnp.concatenate([value, other]), jnp.concatenate([other, value]))

    def reduce_small(value):
        if not grid_like:
            return lax.psum(value, ("chip", "core", "sp"))
        value = value + swap(value)
        value = value + plane(value, 0)
        value = value + plane(value, 1)
        value = value + lax.ppermute(value, "sp", near)
        return value + lax.ppermute(value, "sp", apart)

    vectors = [first_gain, first_shift, query_bias, value_bias, output_bias, second_gain, second_shift,
               reduce_bias, expand_bias]
    small = jnp.concatenate(vectors)
    small_row = jnp.pad(small[None, :], ((0, 15), (0, 3 * group - small.shape[0])))
    if grid_like:
        send0, send1, a_mine, a_part, b_mine, b_part = kernel_call(
            prep_kernel,
            [((local + 16, width), bf16)] * 2 + [((own_rows + 16, 3 * group), bf16)] * 2
            + [((own_rows, width + hidden), bf16)] * 2,
            (tab, inputs, block_ids.astype(f32), w_project, w_output, w_expand, small_row),
            moved=2**22,
            name="prep",
        )
    else:
        id_rows = jnp.pad(block_ids.astype(bf16)[:, None, :], ((0, 0), (0, 15), (0, width - local)))
        packed = jnp.concatenate([inputs, id_rows], axis=1)
        send0, send1 = pick(packed, parity), pick(packed, 1 - parity)

        def halves(target):
            wp = lax.dynamic_index_in_dim(w_project.reshape(own_rows, 3, 2, group), target, 2, False)
            we = lax.dynamic_index_in_dim(
                w_expand.reshape(own_rows, chips, 2, own_hidden), target, 2, False
            )
            return wp.reshape(own_rows, 3 * group), jnp.concatenate([w_output, we.reshape(own_rows, hidden)], axis=1)

        a_mine, b_mine = halves(core)
        a_part, b_part = halves(1 - core)

    got_a = swap(a_part)
    p0, p1 = to_sequence((send0, send1))
    got_b = swap(b_part)

    def ordered(mine, other):
        return jnp.where(core == 0, jnp.concatenate([mine, other]), jnp.concatenate([other, mine]))

    block_a = ordered(a_mine, got_a)
    a_pieces = gather(block_a)
    step_a = block_a.shape[0] // 2
    if grid_like:
        shown = [p[side * step_a + own_rows] for p in (a_pieces[0], a_pieces[2], a_pieces[1], a_pieces[3]) for side in range(2)]
        shown = jnp.stack(shown).reshape(PARTS, 2, -1)
        hot = (order[None, :] == jnp.arange(PARTS)[:, None])[:, :, None, None]
        small_all = jnp.sum(jnp.where(hot, shown[None].astype(f32), 0.0), axis=1).reshape(2 * chips, -1)
    else:
        both_small = lax.all_gather(small_row[:1], ("chip", "core"), axis=0, tiled=True)
        small_all = both_small.astype(f32)
    vec = jnp.transpose(small_all[:, : 8 * own_rows].reshape(2 * chips, 8, own_rows), (1, 0, 2)).reshape(8, width)
    ebias = lax.dynamic_index_in_dim(
        small_all[:, 8 * own_rows : 8 * own_rows + own_hidden].reshape(chips, 2, own_hidden), core, 1, False
    ).reshape(1, hidden)

    q0, q1 = swap(p0), swap(p1)
    block_b = after(ordered(b_mine, got_b), a_pieces[1])
    b_pieces = gather(block_b)
    r_pieces = gather(after(w_reduce, b_pieces[1]))
    late_grad = after(out_grad, a_pieces[3])
    g0, g1 = to_sequence((pick(late_grad, parity), pick(late_grad, 1 - parity)))
    h0, h1 = swap(g0), swap(g1)

    att, qkv0, qkv1, qkv2, lse, normed_t, wp0, wp1, wp2, masks = kernel_call(
        attend_kernel,
        [((rows, group), bf16)] + [((3, rows, 2 * HD), bf16)] * 3 + [((8, rows), f32), ((width, rows), bf16)]
        + [((width, pair_w), bf16)] * 3 + [((rows, 2 * HD), bf16)],
        (tab, p0, p1, q0, q1, *a_pieces, vec),
        [((width, 3 * group), bf16), ((rows, width), bf16), ((per_dev, rows, 2 * HD), bf16),
         ((per_dev, rows, 2 * HD), bf16), ((per_dev, rows, HD), bf16), ((per_dev, rows, HD), bf16),
         ((rows, 128), f32)],
        flops=20 * 10**9,
        moved=2**23,
        name="attend",
    )
    att_oth = swap(att)
    middle, nm_own, *wo_rows = kernel_call(
        mix_kernel,
        [((half, width), f32), ((half, width), bf16)] + [((2 * HD, width), bf16)] * 3,
        (tab, p0, p1, att, att_oth, *b_pieces, vec),
        [((width, width), bf16)],
        flops=4 * 10**9,
        moved=2**23,
        name="mix",
    )
    nm_oth = swap(nm_own)
    (out_own, out_oth, dy_own, dy_oth, red_keep, red_send, exp_keep, exp_send, ebias_sum) = kernel_call(
        feed_kernel,
        [((half, width), f32), ((half, width), bf16), ((half, width), f32), ((half, width), bf16),
         ((2, block, width), bf16), ((2, block, width), bf16), ((2, piece, hidden), bf16),
         ((2, piece, hidden), bf16), ((1, hidden), f32)],
        (tab, nm_own, nm_oth, g0, g1, h0, h1, *b_pieces, *r_pieces, ebias),
        [((rows, width), bf16), ((rows, width), bf16), ((width, hidden), bf16), ((rows, width), f32),
         ((rows, width), f32)],
        flops=25 * 10**9,
        moved=2**24,
        name="feed",
    )
    dy_in = swap(dy_oth)
    grad_middle, gb_own, sums_two = kernel_call(
        second_kernel,
        [((half, width), f32), ((half, width), bf16), ((8, width), f32)],
        (tab, middle, dy_own, dy_in, g0, g1, vec),
        flops=4 * 10**9,
        moved=2**23,
        name="second",
    )
    gb_oth = swap(gb_own)
    red = plane_one(red_keep, red_send)
    exp = plane_one(exp_keep, exp_send)
    out_in = swap(out_oth)

    def back(pair, more, last=False, tie=()):
        qkv = (qkv0, qkv1, qkv2)[pair]
        wo_pair = wo_rows[pair]
        cols = pair_w if last else (2 + pair) * group
        if last or pair:
            cols = pair_w if last else 3 * group
        outs = [((rows, pair_w), bf16), ((2, piece, cols), bf16), ((2, piece, cols), bf16), ((8, pair_w), f32)]
        if last:
            outs += [((half, width), f32), ((half, width), bf16)]
        source = after(gb_oth, *tie) if tie else gb_oth
        return kernel_call(
            lambda *refs: back_kernel(pair, last, pair, refs),
            outs,
            (tab, gb_own, source, wo_pair, qkv, lse, masks, normed_t, *more),
            [((rows, width), bf16), ((2, rows, 2 * HD), bf16), ((2, rows, 2 * HD), bf16), ((2, HD, rows), bf16),
             ((2, rows, 2 * HD), bf16), ((2, rows, HD), f32), ((2, rows, HD), f32), ((2, rows, HD), f32)],
            flops=10 * 10**9,
            moved=2**23,
            name="back",
        )

    dproj0, keep0, send0, sums_p0 = back(0, (att, att_oth), tie=(red,))
    red = plane_two(red)
    dproj1, keep1, send1, sums_p1 = back(1, (keep0, send0), tie=(exp, red))
    exp = plane_two(exp)
    red = line_one(red)
    part = plane_one(keep1, send1)
    dproj2, keep2, send2, sums_p2, dx_own, dx_oth = back(
        2, (dproj0, dproj1, wp0, wp1, wp2), last=True, tie=(exp, red)
    )
    dx_in = swap(dx_oth)
    tail = plane_one(keep2, send2)
    red = line_two(red)
    exp = line_one(exp)
    result = (middle + (out_own + out_in.astype(f32) + vec[7:8, :])).astype(bf16)
    layer_output = from_sequence((result[:local], result[local:]))
    grad_in0, grad_in1, sums_one = kernel_call(
        first_kernel,
        [((local, width), bf16), ((local, width), bf16), ((8, width), f32)],
        (tab, p0, p1, dx_own, dx_in, grad_middle, vec),
        flops=4 * 10**9,
        moved=2**22,
        name="first",
    )
    input_grad = from_sequence((grad_in0, grad_in1)).astype(f32)
    part = plane_two(part)
    exp = line_two(exp)
    red = line_four(line_three(red))
    exp = line_four(line_three(exp))
    part = line_four(line_three(line_two(line_one(part))))
    tail = plane_two(tail)
    tail = added(tail, lax.ppermute(tail, "sp", near))
    tail = added(tail, lax.ppermute(tail, "sp", apart))

    def spread(values):
        value = jnp.concatenate(values)
        zero = jnp.zeros_like(value)
        return jnp.where(core == 0, jnp.concatenate([value, zero]), jnp.concatenate([zero, value]))

    pair_sums = (sums_p0[0], sums_p1[0], sums_p2[0])
    owners = 2 * chips
    sums = jnp.stack(
        [spread([p[: 2 * HD] for p in pair_sums]), spread([p[4 * HD :] for p in pair_sums]),
         sums_two[2], sums_two[0], sums_two[1], sums_two[3]]
    )
    sums = jnp.concatenate([sums_one[:2], sums])
    table = jnp.transpose(sums.reshape(8, owners, own_rows), (1, 0, 2)).reshape(owners, 8 * own_rows)
    eb = jnp.where(jnp.arange(2)[None, :, None] == core, ebias_sum.reshape(chips, 1, own_hidden), 0.0)
    table = jnp.concatenate([table, eb.reshape(owners, own_hidden)], axis=1)
    small_sum = pick(reduce_small(table), 2 * chip + core)

    def mine_of(value, target):
        return lax.dynamic_slice_in_dim(value, target * own_rows, own_rows, 0)

    def both(value):
        mine, other = mine_of(value, core), swap(mine_of(value, 1 - core))
        return jnp.where(core == 0, jnp.stack([mine, other]), jnp.stack([other, mine])).astype(f32)

    exp_both, part_both, tail_both = both(exp), both(part), both(tail)
    grad_expand = jnp.transpose(
        exp_both.reshape(2, own_rows, chips, own_hidden), (1, 2, 0, 3)
    ).reshape(own_rows, -1)
    grad_output = jnp.transpose(part_both[:, :, :group], (1, 0, 2)).reshape(own_rows, width)
    grad_project = jnp.concatenate([part_both[:, :, group:], tail_both], axis=2)
    grad_project = jnp.transpose(
        grad_project.reshape(2, own_rows, pairs_dev, 3, 2 * HD), (1, 3, 0, 2, 4)
    ).reshape(own_rows, -1)
    cut = [small_sum[i * own_rows : (i + 1) * own_rows] for i in range(8)]
    return (
        layer_output,
        input_grad,
        cut[0],
        cut[1],
        grad_project,
        cut[2],
        cut[3],
        grad_output,
        cut[4],
        cut[5],
        cut[6],
        grad_expand,
        small_sum[8 * own_rows : 8 * own_rows + own_hidden],
        red.astype(f32),
        cut[7],
    )


def solution(mesh):
    owners, groups = mesh.shape["fsdp"], mesh.shape["sp"]
    split = Mesh(mesh.devices.reshape(owners // 2, 2, groups), ("chip", "core", "sp"))
    own = ("chip", "core")
    rows, flat, both = P(own, None), P(own), P(own, "sp", None)
    return jax.shard_map(
        per_device,
        mesh=split,
        in_specs=(both, P(own, "sp"), flat, flat, rows, flat, flat, rows, flat, flat, flat, rows, flat,
                  rows, flat, both),
        out_specs=(both, both, flat, flat, rows, flat, flat, rows, flat, flat, flat, rows, flat, rows, flat),
        check_vma=False,
    )
```

```python
import math

import jax
import jax.numpy as jnp
from jax import lax
from jax.experimental import pallas as pl
from jax.experimental.pallas import tpu as pltpu
from jax.sharding import Mesh, PartitionSpec as P


HD = 64
EPSILON = 1e-05
GELU_C = 0.7978845608028654
GELU_A = 0.044715
MASKED = -1e30
SCALE = 1.0 / math.sqrt(HD)
PARTS = 4
TILE = 256
f32 = jnp.float32
bf16 = jnp.bfloat16
VM = pl.BlockSpec(memory_space=pltpu.VMEM)
SM = pl.BlockSpec(memory_space=pltpu.SMEM)


def dot(left, right, left_dim, right_dim):
    return lax.dot_general(
        left, right, (((left_dim,), (right_dim,)), ((), ())), preferred_element_type=f32
    )


def kernel_call(body, outs, args, scratch=(), flops=0, moved=0):
    return pl.pallas_call(
        body,
        out_shape=[jax.ShapeDtypeStruct(s, d) for s, d in outs],
        in_specs=[SM] + [VM] * (len(args) - 1),
        out_specs=[VM] * len(outs),
        scratch_shapes=[pltpu.VMEM(s, d) for s, d in scratch],
        compiler_params=pltpu.CompilerParams(vmem_limit_bytes=58 * 2**20),
        cost_estimate=pl.CostEstimate(flops=flops, bytes_accessed=moved, transcendentals=0),
    )(*args)


def normalize(rows):
    average = jnp.mean(rows, axis=-1, keepdims=True)
    centered = rows - average
    variance = jnp.mean(centered * centered, axis=-1, keepdims=True)
    inv_std = lax.rsqrt(variance + EPSILON)
    return centered * inv_std, inv_std


def norm_backward(grad_rows, normed, inv_std, gain):
    scaled = grad_rows * gain
    first_mean = jnp.mean(scaled, axis=-1, keepdims=True)
    second_mean = jnp.mean(scaled * normed, axis=-1, keepdims=True)
    return inv_std * (scaled - first_mean - normed * second_mean)


def gelu_parts(pre):
    square = pre * pre
    tangent = jnp.tanh(GELU_C * (pre + GELU_A * pre * square))
    half = 0.5 * (1.0 + tangent)
    value = pre * half
    slope = half + 0.5 * pre * (1.0 - tangent * tangent) * GELU_C * (1.0 + 3.0 * GELU_A * square)
    return value, slope


def offset(index, step):
    return pl.multiple_of(index * step, step)


def prep_kernel(tab, x, ids, wp, wo, we, small, send0, send1, a_mine, a_part, b_mine, b_part):
    local, width = x.shape[1:]
    rows = wp.shape[0]
    core, par = tab[0], tab[5]
    group = width // 2
    for turn, out in enumerate((send0, send1)):
        which = lax.rem(par + turn, 2)
        out[:local, :] = x[which]
        line = jnp.where(which == 0, ids[0:1, :], ids[1:2, :])
        out[local:, :] = jnp.zeros((16, width), bf16)
        out[local:, :local] = jnp.broadcast_to(line.astype(f32), (16, local)).astype(bf16)
    for out, place in ((a_mine, core), (a_part, 1 - core)):
        for part in range(3):
            out[:rows, part * group : (part + 1) * group] = wp[
                :, pl.ds(pl.multiple_of(part * width + place * group, group), group)
            ]
        out[rows:, :] = small[...]
    for out, place in ((b_mine, core), (b_part, 1 - core)):
        out[:, :width] = wo[...]
        block = we.shape[1] // (2 * PARTS)
        for chip in range(PARTS):
            out[:, width + chip * block : width + (chip + 1) * block] = we[
                :, pl.ds(pl.multiple_of((2 * chip + place) * block, block), block)
            ]


def fill(target, pieces, tab, cols, piece):
    own, one, two, far = pieces
    step = own.shape[0] // 2
    seg = piece // 2
    for rel, ref in enumerate((own, two, one, far)):
        for side in range(2):
            target[pl.ds(pl.multiple_of(tab[1 + rel] * piece + side * seg, seg), seg), :] = ref[
                side * step : side * step + seg, cols
            ]


def natural(tab, place, turn, local):
    return pl.ds(pl.multiple_of(place * 2 * local + lax.rem(tab[5] + turn, 2) * local, local), local)


def project_kernel(
    tab, p0, p1, q0, q1, w_own, w_one, w_two, w_far, vec,
    qkv0, qkv1, qkv2, normed_t, wp0, wp1, wp2, masks, w_nat, normed,
):
    local = p0.shape[0] - 16
    width = normed.shape[1]
    group = width // 2
    core = tab[0]
    fill(w_nat, (w_own, w_one, w_two, w_far), tab, slice(None), width // PARTS)
    gain, shift = vec[0:1, :], vec[1:2, :]
    lane = lax.broadcasted_iota(jnp.int32, (local, HD), 1).astype(f32)
    for place, refs in ((core, (p0, p1)), (1 - core, (q0, q1))):
        for turn, ref in enumerate(refs):
            span = natural(tab, place, turn, local)
            full, _ = normalize(ref[:local, :].astype(f32))
            normed[span, :] = (full * gain + shift).astype(bf16)
            line = jnp.broadcast_to(ref[local : local + 1, :local].astype(f32), (128, local))
            own = jnp.transpose(line)[:, :HD]
            masks[span, :] = jnp.concatenate(
                [
                    jnp.where((lane > own) & (lane < 4.0), MASKED, 0.0).astype(bf16),
                    jnp.where(lane == own, 1.0, 0.0).astype(bf16),
                ],
                axis=1,
            )
    own_cols = pl.ds(offset(core, group), group)
    biases = (vec[2:3, own_cols], None, vec[3:4, own_cols])
    for pair in range(group // (2 * HD)):
        qkv, wp = (qkv0, qkv1, qkv2)[pair], (wp0, wp1, wp2)[pair]
        for part in range(3):
            col = part * group + pair * 2 * HD
            weights = w_nat[:, col : col + 2 * HD]
            wp[:, part * 2 * HD : (part + 1) * 2 * HD] = weights
            low = dot(normed[...], weights, 1, 0)
            if biases[part] is not None:
                low = low + biases[part][:, pair * 2 * HD : (pair + 1) * 2 * HD]
            qkv[part] = low.astype(bf16)
    normed_t[...] = jnp.transpose(normed[...])


def attend_kernel(tab, *refs):
    pairs = len(refs) - 8
    masks, qkvs = refs[0], refs[1:pairs + 1]
    att, lse, qa, ka, va, mixed, lcol = refs[pairs + 1 :][:7]
    rows = att.shape[0]
    for pair in range(pairs):
        for side in range(2):
            span = slice(side * HD, (side + 1) * HD)
            head = 2 * pair + side
            qa[head] = jnp.concatenate(
                [qkvs[pair][0, :, span] * jnp.asarray(SCALE, bf16), masks[:, :HD]], axis=1
            )
            ka[head] = jnp.concatenate([qkvs[pair][1, :, span], masks[:, HD:]], axis=1)
            va[head] = qkvs[pair][2, :, span]
    wide = lax.broadcasted_iota(jnp.int32, (TILE, 128), 1)

    def one_head(head, carry):
        for tile in range(rows // TILE):
            span = slice(tile * TILE, (tile + 1) * TILE)
            scores = dot(qa[head, span, :], ka[head], 1, 1)
            peak = jnp.max(scores, axis=1, keepdims=True)
            raised = jnp.exp(scores - peak)
            summed = jnp.sum(raised, axis=1, keepdims=True)
            out = dot(raised.astype(bf16), va[head], 1, 0) / summed
            mixed[head, span, :] = out.astype(bf16)
            lcol[span, :] = jnp.where(
                wide == head, jnp.broadcast_to(peak + jnp.log(summed), (TILE, 128)), lcol[span, :]
            )
        return carry

    lcol[...] = jnp.zeros_like(lcol)
    lax.fori_loop(0, 2 * pairs, one_head, 0)
    for pair in range(pairs):
        att[:, pair * 2 * HD : (pair + 1) * 2 * HD] = jnp.concatenate(
            [mixed[2 * pair], mixed[2 * pair + 1]], axis=1
        )
    lse[...] = jnp.transpose(lcol[...])[:8, :]


def mix_kernel(
    tab, p0, p1, own_a, own_b, oth_a, oth_b, w_own, w_one, w_two, w_far, vec,
    middle, normed, wo0, wo1, wo2, w_nat,
):
    local = p0.shape[0] - 16
    width = w_nat.shape[1]
    group = width // 2
    cut = own_a.shape[1]
    core = tab[0]
    fill(w_nat, (w_own, w_one, w_two, w_far), tab, slice(0, width), width // PARTS)
    mine = w_nat[pl.ds(offset(core, group), group), :]
    theirs = w_nat[pl.ds(offset(1 - core, group), group), :]
    for turn, ref in enumerate((p0, p1)):
        span = natural(tab, core, turn, local)
        total = ref[:local, :].astype(f32) + (
            dot(own_a[span, :], mine[:cut], 1, 0)
            + dot(own_b[span, :], mine[cut:], 1, 0)
            + dot(oth_a[span, :], theirs[:cut], 1, 0)
            + dot(oth_b[span, :], theirs[cut:], 1, 0)
            + vec[4:5, :]
        )
        place = slice(turn * local, (turn + 1) * local)
        middle[place, :] = total
        full, _ = normalize(total)
        normed[place, :] = (full * vec[5:6, :] + vec[6:7, :]).astype(bf16)
    for pair, ref in enumerate((wo0, wo1, wo2)):
        ref[...] = mine[pair * 2 * HD : (pair + 1) * 2 * HD, :]


def scatter_rows(value, tab, piece, keep, send, cols=slice(None), place=slice(None)):
    for chip in range(PARTS):
        rows = value[chip * piece : (chip + 1) * piece, :]
        for target in range(PARTS):

            @pl.when(tab[1 + target] == chip)
            def _():
                if target < 2:
                    keep[target, place, cols] = rows
                else:
                    send[target - 2, place, cols] = rows


def feed_kernel(
    tab, nm_own, nm_oth, g0, g1, h0, h1, e_own, e_one, e_two, e_far, r_own, r_one, r_two, r_far, ebias,
    out_own, out_oth, dy_own, dy_oth, keep, send, bias_sum,
    nm, gt, we, out_acc, dy_acc,
):
    half, width = nm_own.shape
    local = half // 2
    block = r_own.shape[0]
    piece = width // PARTS
    hidden = PARTS * block
    nm[:half, :] = nm_own[...]
    nm[half:, :] = nm_oth[...]
    for index, ref in enumerate((g0, g1, h0, h1)):
        gt[index * local : (index + 1) * local, :] = ref[...]
    fill(we, (e_own, e_one, e_two, e_far), tab, slice(width, width + hidden), width // PARTS)
    for rel in range(PARTS):
        place = pl.ds(offset(tab[1 + rel], block), block)
        w_red = (r_own, r_two, r_one, r_far)[rel][...]
        w_exp = we[:, place]
        pre = dot(nm[...], w_exp, 1, 0) + ebias[:, place]
        value, slope = gelu_parts(pre)
        active = value.astype(bf16)
        part_out = dot(active, w_red, 1, 0)
        grad_red = dot(active, gt[...], 0, 0).astype(bf16)
        if rel < 2:
            keep[rel, :block, :] = grad_red
        else:
            send[rel - 2, :block, :] = grad_red
        grad_hidden = (dot(gt[...], w_red, 1, 1) * slope).astype(bf16)
        bias_sum[:, place] = jnp.sum(grad_hidden.astype(f32), axis=0, keepdims=True)
        grad_exp = dot(nm[...], grad_hidden, 0, 0).astype(bf16)
        target_cols = pl.ds(offset(lax.rem(tab[1 + rel], 2), block), block)
        target_rows = pl.ds(pl.multiple_of(block + (tab[1 + rel] // 2) * piece, piece), piece)
        scatter_rows(grad_exp, tab, piece, keep, send, target_cols, target_rows)
        part_dy = dot(grad_hidden, w_exp, 1, 1)
        if rel == 0:
            out_acc[...] = part_out
            dy_acc[...] = part_dy
        else:
            out_acc[...] += part_out
            dy_acc[...] += part_dy
    out_own[...] = out_acc[:half, :]
    out_oth[...] = out_acc[half:, :].astype(bf16)
    dy_own[...] = dy_acc[:half, :]
    dy_oth[...] = dy_acc[half:, :].astype(bf16)


def second_kernel(tab, middle, dy_own, dy_in, g0, g1, vec, grad_middle, branch, sums):
    local = g0.shape[0]
    sums[...] = jnp.zeros_like(sums)
    for turn, ref in enumerate((g0, g1)):
        span = slice(turn * local, (turn + 1) * local)
        grad_rows = dy_own[span, :] + dy_in[span, :].astype(f32)
        full, inv_std = normalize(middle[span, :])
        top = ref[...].astype(f32)
        total = top + norm_backward(grad_rows, full, inv_std, vec[5:6, :])
        low = total.astype(bf16)
        grad_middle[span, :] = total
        branch[span, :] = low
        sums[0:1, :] += jnp.sum(grad_rows * full, axis=0, keepdims=True)
        sums[1:2, :] += jnp.sum(grad_rows, axis=0, keepdims=True)
        sums[2:3, :] += jnp.sum(low.astype(f32), axis=0, keepdims=True)
        sums[3:4, :] += jnp.sum(top, axis=0, keepdims=True)


def back_kernel(pair, last, extra, refs):
    tab, gb_own, gb_oth, wo_pair, qkv, lse, masks, normed_t = refs[:8]
    refs = refs[8:]
    if extra == 0:
        atts = refs[:4]
        refs = refs[4:]
    else:
        old_keep, old_send = (refs[0], refs[1]) if not last else (None, None)
        refs = refs if last else refs[2:]
    dproj, keep, send, sums = refs[:4]
    refs = refs[4:]
    gb, qa, ka, kt, do, dq, dk, dv = refs
    half, width = gb_own.shape
    local = half // 2
    rows = 2 * half
    piece = keep.shape[1]
    group = width // 2
    core = tab[0]
    for place, ref in ((core, gb_own), (1 - core, gb_oth)):
        for turn in range(2):
            gb[natural(tab, place, turn, local), :] = ref[turn * local : (turn + 1) * local, :]
    pair_w = 2 * HD
    grad_att = dot(gb[...], wo_pair[...], 1, 1).astype(bf16)
    keys_t = jnp.transpose(qkv[1])
    for side in range(2):
        span = slice(side * HD, (side + 1) * HD)
        qa[side] = jnp.concatenate([qkv[0, :, span] * jnp.asarray(SCALE, bf16), masks[:, :HD]], axis=1)
        ka[side] = jnp.concatenate([qkv[1, :, span], masks[:, HD:]], axis=1)
        kt[side] = keys_t[span, :]
        do[side] = jnp.concatenate([grad_att[:, span], qkv[2, :, span]], axis=1)

    def one_head(side, carry):
        values = do[side][:, HD:]
        for tile in range(rows // TILE):
            span = slice(tile * TILE, (tile + 1) * TILE)
            query = qa[side, span, :]
            grad_mix = do[side, span, :HD]
            scores = dot(ka[side], query, 1, 1)
            prob = jnp.exp(scores - lse[pl.ds((0 if last else 2 * pair) + side, 1), span])
            grad_prob = dot(values, grad_mix, 1, 1)
            centre = jnp.sum(prob * grad_prob, axis=0, keepdims=True)
            grad_scores = (prob * (grad_prob - centre)).astype(bf16)
            part_v = dot(prob.astype(bf16), grad_mix, 1, 0)
            part_k = dot(grad_scores, query, 1, 0)[:, :HD]
            part_q = dot(kt[side], grad_scores, 1, 0) * SCALE
            dq[side, span, :] = jnp.transpose(part_q)
            if tile == 0:
                dv[side] = part_v
                dk[side] = part_k
            else:
                dv[side] += part_v
                dk[side] += part_k
        return carry

    lax.fori_loop(0, 2, one_head, 0)
    for part, ref in enumerate((dq, dk, dv)):
        low = jnp.concatenate([ref[0], ref[1]], axis=1).astype(bf16)
        span = slice(part * pair_w, (part + 1) * pair_w)
        dproj[:, span] = low
        sums[:, span] = jnp.broadcast_to(jnp.sum(low.astype(f32), axis=0, keepdims=True), (8, pair_w))
    grad = dot(normed_t[...], dproj[...], 1, 0).astype(bf16)
    if last:
        scatter_rows(grad, tab, piece, keep, send)
    elif extra == 0:
        scatter_rows(grad, tab, piece, keep, send, slice(group, 2 * group))
        gb_cols = gb[:, pl.ds(offset(core, group), group)]
        first, second = [
            jnp.concatenate([dot(ref[...], gb_cols, 0, 0) for ref in two], axis=0).astype(bf16)
            for two in (atts[:2], atts[2:])
        ]
        low_rows = jnp.where(core == 0, first, second)
        high_rows = jnp.where(core == 0, second, first)
        scatter_rows(jnp.concatenate([low_rows, high_rows], axis=0), tab, piece, keep, send, slice(0, group))
    else:
        keep[:, :, : 2 * group] = old_keep[...]
        send[:, :, : 2 * group] = old_send[...]
        scatter_rows(grad, tab, piece, keep, send, slice(2 * group, 3 * group))


def source_kernel(tab, dproj0, dproj1, dproj2, wp0, wp1, wp2, dx_own, dx_oth):
    half = dx_own.shape[0]
    local = half // 2
    for place, out in ((1 - tab[0], dx_oth), (tab[0], dx_own)):
        for turn in range(2):
            span = natural(tab, place, turn, local)
            total = dot(dproj0[span, :], wp0[...], 1, 1)
            total = total + dot(dproj1[span, :], wp1[...], 1, 1)
            total = total + dot(dproj2[span, :], wp2[...], 1, 1)
            out[turn * local : (turn + 1) * local, :] = total.astype(out.dtype)


def first_kernel(tab, p0, p1, dy_own, dy_in, grad_middle, vec, out0, out1, sums):
    local = out0.shape[0]
    sums[...] = jnp.zeros_like(sums)
    for turn, (ref, out) in enumerate(((p0, out0), (p1, out1))):
        span = slice(turn * local, (turn + 1) * local)
        grad_rows = dy_own[span, :] + dy_in[span, :].astype(f32)
        full, inv_std = normalize(ref[:local, :].astype(f32))
        total = grad_middle[span, :] + norm_backward(grad_rows, full, inv_std, vec[0:1, :])
        out[...] = total.astype(bf16)
        sums[0:1, :] += jnp.sum(grad_rows * full, axis=0, keepdims=True)
        sums[1:2, :] += jnp.sum(grad_rows, axis=0, keepdims=True)


def after(value, *others):
    return lax.optimization_barrier((value, *others))[0]


def layer(
    inputs, block_ids, first_gain, first_shift, w_project, query_bias, value_bias, w_output,
    output_bias, second_gain, second_shift, w_expand, expand_bias, w_reduce, reduce_bias, out_grad,
):
    _, local, width = inputs.shape
    chips = lax.axis_size("chip")
    groups = lax.axis_size("sp")
    half = 2 * local
    rows = 2 * half
    group = width // 2
    own_rows = w_project.shape[0]
    own_hidden = w_reduce.shape[0]
    hidden = chips * own_hidden
    piece = width // PARTS
    block = hidden // PARTS
    per_dev = group // HD
    pairs_dev = per_dev // 2
    pair_w = 6 * HD
    core = lax.axis_index("core")
    chip = lax.axis_index("chip")
    zed = lax.axis_index("sp")
    parity = lax.rem(zed, 2)
    grid_like = chips == PARTS
    swap_pairs = [(0, 1), (1, 0)]

    def swap(value):
        return lax.ppermute(value, "core", swap_pairs)

    def seq_pairs(turn):
        return [
            (c * groups + z, (z // 2) * groups + 2 * c + (z + turn) % 2)
            for c in range(2)
            for z in range(groups)
        ]

    def to_sequence(pieces):
        return [lax.ppermute(pieces[turn], ("core", "sp"), seq_pairs(turn)) for turn in range(2)]

    def from_sequence(pieces):
        got = [
            lax.ppermute(pieces[turn], ("core", "sp"), [(b, a) for a, b in seq_pairs(turn)])
            for turn in range(2)
        ]
        return jnp.stack(
            [jnp.where(parity == 0, got[0], got[1]), jnp.where(parity == 0, got[1], got[0])]
        )

    def plane(value, step):
        pairs = []
        for i in range(PARTS):
            for c in range(2):
                flip = (1, 2)[c] if step == 0 else (2, 1)[c]
                pairs.append((i * 2 + c, (i ^ flip) * 2 + c))
        return lax.ppermute(value, ("chip", "core"), pairs)

    if grid_like:
        flips = jnp.where(core == 0, jnp.array([0, 2, 1, 3]), jnp.array([0, 1, 2, 3]))
        order = (chip ^ flips).astype(jnp.int32)
    else:
        order = jnp.arange(PARTS, dtype=jnp.int32)
    tab = jnp.concatenate([core[None].astype(jnp.int32), order, parity[None].astype(jnp.int32)])

    def gather(value):
        if grid_like:
            one = plane(value, 0)
            return value, one, plane(value, 1), plane(one, 1)
        full = lax.all_gather(value, "chip", axis=0, tiled=True)
        full = full.reshape(PARTS, full.shape[0] // PARTS, full.shape[1])
        return full[0], full[2], full[1], full[3]

    def added(left, right):
        return (left.astype(f32) + right.astype(f32)).astype(bf16)

    def plane_one(keep, send):
        if grid_like:
            return added(keep, plane(send, 0))
        full = jnp.concatenate([keep, send]).reshape(-1, keep.shape[2])
        return lax.psum_scatter(full, "chip", scatter_dimension=0, tiled=True)

    def plane_two(total):
        return added(total[0], plane(total[1], 1)) if grid_like else total

    near = [(z, z ^ 1) for z in range(groups)]
    apart = [(z, z ^ 2) for z in range(groups)]
    low_bit, high_bit = lax.rem(zed, 2), zed // 2

    def pick(value, index):
        return lax.dynamic_index_in_dim(value, index, 0, False)

    def line_one(value):
        cut = value.reshape(2, 2, value.shape[0] // 4, value.shape[1])
        return added(pick(cut, low_bit), lax.ppermute(pick(cut, 1 - low_bit), "sp", near))

    def line_two(value):
        return added(pick(value, high_bit), lax.ppermute(pick(value, 1 - high_bit), "sp", apart))

    def line_three(value):
        other = lax.ppermute(value, "sp", apart)
        return jnp.where(high_bit == 0, jnp.concatenate([value, other]), jnp.concatenate([other, value]))

    def line_four(value):
        other = lax.ppermute(value, "sp", near)
        return jnp.where(low_bit == 0, jnp.concatenate([value, other]), jnp.concatenate([other, value]))

    def reduce_small(value):
        if not grid_like:
            return lax.psum(value, ("chip", "core", "sp"))
        value = value + swap(value)
        value = value + plane(value, 0)
        value = value + plane(value, 1)
        value = value + lax.ppermute(value, "sp", near)
        return value + lax.ppermute(value, "sp", apart)

    vectors = [first_gain, first_shift, query_bias, value_bias, output_bias, second_gain, second_shift,
               reduce_bias, expand_bias]
    small_row, start = None, 0
    for vector in vectors:
        end = start + vector.shape[0]
        placed = jnp.pad(vector[None, :].astype(f32), ((0, 15), (start, 3 * group - end)))
        small_row = placed if small_row is None else small_row + placed
        start = end
    small_row = small_row.astype(bf16)
    if grid_like:
        send0, send1, a_mine, a_part, b_mine, b_part = kernel_call(
            prep_kernel,
            [((local + 16, width), bf16)] * 2 + [((own_rows + 16, 3 * group), bf16)] * 2
            + [((own_rows, width + hidden), bf16)] * 2,
            (tab, inputs, block_ids, w_project, w_output, w_expand, small_row),
            moved=2**22,
        )
    else:
        id_rows = jnp.pad(block_ids.astype(bf16)[:, None, :], ((0, 0), (0, 15), (0, width - local)))
        packed = jnp.concatenate([inputs, id_rows], axis=1)
        send0, send1 = pick(packed, parity), pick(packed, 1 - parity)

        def halves(target):
            wp = lax.dynamic_index_in_dim(w_project.reshape(own_rows, 3, 2, group), target, 2, False)
            we = lax.dynamic_index_in_dim(
                w_expand.reshape(own_rows, chips, 2, own_hidden), target, 2, False
            )
            return wp.reshape(own_rows, 3 * group), jnp.concatenate([w_output, we.reshape(own_rows, hidden)], axis=1)

        a_mine, b_mine = halves(core)
        a_part, b_part = halves(1 - core)

    got_a = swap(a_part)
    p0, p1 = to_sequence((send0, send1))
    got_b = swap(b_part)

    def ordered(mine, other):
        return jnp.where(core == 0, jnp.concatenate([mine, other]), jnp.concatenate([other, mine]))

    block_a = ordered(a_mine, got_a)
    a_pieces = gather(block_a)
    step_a = block_a.shape[0] // 2
    if grid_like:
        shown = [p[side * step_a + own_rows] for p in (a_pieces[0], a_pieces[2], a_pieces[1], a_pieces[3]) for side in range(2)]
        shown = jnp.stack(shown).reshape(PARTS, 2, -1)
        hot = (order[None, :] == jnp.arange(PARTS)[:, None])[:, :, None, None]
        small_all = jnp.sum(jnp.where(hot, shown[None].astype(f32), 0.0), axis=1).reshape(2 * chips, -1)
    else:
        both_small = lax.all_gather(small_row[:1], ("chip", "core"), axis=0, tiled=True)
        small_all = both_small.astype(f32)
    vec = jnp.transpose(small_all[:, : 8 * own_rows].reshape(2 * chips, 8, own_rows), (1, 0, 2)).reshape(8, width)
    ebias = lax.dynamic_index_in_dim(
        small_all[:, 8 * own_rows : 8 * own_rows + own_hidden].reshape(chips, 2, own_hidden), core, 1, False
    ).reshape(1, hidden)

    q0, q1 = swap(p0), swap(p1)
    late_grad = after(out_grad, p0, p1)
    g0, g1 = to_sequence((pick(late_grad, parity), pick(late_grad, 1 - parity)))
    block_b = after(ordered(b_mine, got_b), a_pieces[3])
    b_pieces = gather(block_b)

    qkv0, qkv1, qkv2, normed_t, wp0, wp1, wp2, masks = kernel_call(
        project_kernel,
        [((3, rows, 2 * HD), bf16)] * 3 + [((width, rows), bf16)] + [((width, pair_w), bf16)] * 3
        + [((rows, 2 * HD), bf16)],
        (tab, p0, p1, q0, q1, *a_pieces, vec),
        [((width, 3 * group), bf16), ((rows, width), bf16)],
        flops=6 * 10**9,
        moved=2**23,
    )

    def attend(qkvs):
        heads = 2 * len(qkvs)
        return kernel_call(
            attend_kernel,
            [((rows, heads * HD), bf16), ((8, rows), f32)],
            (tab, masks, *qkvs),
            [((heads, rows, 2 * HD), bf16), ((heads, rows, 2 * HD), bf16), ((heads, rows, HD), bf16),
             ((heads, rows, HD), bf16), ((rows, 128), f32)],
            flops=heads * 3 * 10**9,
            moved=2**22,
        )

    att_a, lse_a = attend((qkv0, qkv1))
    oth_a = swap(att_a)
    r_pieces = gather(after(w_reduce, att_a))
    att_b, lse_b = attend((after(qkv2, att_a),))
    oth_b = swap(att_b)
    h0, h1 = [swap(after(g, att_b)) for g in (g0, g1)]
    middle, nm_own, *wo_rows = kernel_call(
        mix_kernel,
        [((half, width), f32), ((half, width), bf16)] + [((2 * HD, width), bf16)] * 3,
        (tab, p0, p1, att_a, att_b, oth_a, oth_b, *b_pieces, vec),
        [((width, width), bf16)],
        flops=4 * 10**9,
        moved=2**23,
    )
    nm_oth = swap(nm_own)
    out_own, out_oth, dy_own, dy_oth, feed_keep, feed_send, ebias_sum = kernel_call(
        feed_kernel,
        [((half, width), f32), ((half, width), bf16), ((half, width), f32), ((half, width), bf16),
         ((2, 2 * block, width), bf16), ((2, 2 * block, width), bf16), ((1, hidden), f32)],
        (tab, nm_own, nm_oth, g0, g1, h0, h1, *b_pieces, *r_pieces, ebias),
        [((rows, width), bf16), ((rows, width), bf16), ((width, hidden), bf16), ((rows, width), f32),
         ((rows, width), f32)],
        flops=25 * 10**9,
        moved=2**24,
    )
    dy_in = swap(dy_oth)
    grad_middle, gb_own, sums_two = kernel_call(
        second_kernel,
        [((half, width), f32), ((half, width), bf16), ((8, width), f32)],
        (tab, middle, dy_own, dy_in, g0, g1, vec),
        flops=4 * 10**9,
        moved=2**23,
    )
    gb_oth = swap(gb_own)
    if grid_like:
        fed = plane_one(feed_keep, feed_send)
    else:
        whole = jnp.concatenate([feed_keep, feed_send])
        red = lax.psum_scatter(whole[:, :block].reshape(hidden, width), "chip", scatter_dimension=0, tiled=True)
        exp = jnp.transpose(whole[:, block:].reshape(PARTS, 2, piece, width), (0, 2, 1, 3)).reshape(width, hidden)
        exp = lax.psum_scatter(exp, "chip", scatter_dimension=0, tiled=True)
        exp = jnp.transpose(exp.reshape(2 * own_rows, 2, width), (1, 0, 2)).reshape(-1, width)
        fed = jnp.concatenate([red, exp])

    def back(pair, more, last=False, tie=()):
        qkv = (qkv0, qkv1, qkv2)[pair]
        wo_pair = wo_rows[pair]
        cols = pair_w if last else (2 + pair) * group
        if last or pair:
            cols = pair_w if last else 3 * group
        outs = [((rows, pair_w), bf16), ((2, piece, cols), bf16), ((2, piece, cols), bf16), ((8, pair_w), f32)]
        source = after(gb_oth, *tie) if tie else gb_oth
        return kernel_call(
            lambda *refs: back_kernel(pair, last, pair, refs),
            outs,
            (tab, gb_own, source, wo_pair, qkv, lse_b if last else lse_a, masks, normed_t, *more),
            [((rows, width), bf16), ((2, rows, 2 * HD), bf16), ((2, rows, 2 * HD), bf16), ((2, HD, rows), bf16),
             ((2, rows, 2 * HD), bf16), ((2, rows, HD), f32), ((2, rows, HD), f32), ((2, rows, HD), f32)],
            flops=10 * 10**9,
            moved=2**23,
        )

    dproj0, keep0, send0_, sums_p0 = back(0, (att_a, att_b, oth_a, oth_b))
    fed = plane_two(fed)
    out_in = swap(after(out_oth, dproj0))
    result = (middle + (out_own + out_in.astype(f32) + vec[7:8, :])).astype(bf16)
    layer_output = from_sequence((result[:local], result[local:]))
    dproj1, keep1, send1_, sums_p1 = back(1, (keep0, send0_), tie=(dproj0,))
    fed = line_one(fed)
    part = plane_one(keep1, send1_)
    dproj2, keep2, send2_, sums_p2 = back(2, (), last=True, tie=(dproj1,))
    tail = plane_one(keep2, send2_)
    fed = line_two(fed)
    dx_own, dx_oth = kernel_call(
        source_kernel,
        [((half, width), f32), ((half, width), bf16)],
        (tab, dproj0, dproj1, dproj2, wp0, wp1, wp2),
        flops=4 * 10**9,
        moved=2**23,
    )
    dx_in = swap(dx_oth)
    grad_in0, grad_in1, sums_one = kernel_call(
        first_kernel,
        [((local, width), bf16), ((local, width), bf16), ((8, width), f32)],
        (tab, p0, p1, dx_own, dx_in, grad_middle, vec),
        flops=4 * 10**9,
        moved=2**22,
    )
    part = plane_two(part)
    input_grad = from_sequence((grad_in0, grad_in1)).astype(f32)
    fed = line_four(line_three(fed))
    tail = plane_two(tail)
    part = line_four(line_three(line_two(line_one(part))))
    tail = added(tail, lax.ppermute(tail, "sp", near))
    tail = added(tail, lax.ppermute(tail, "sp", apart))
    red = fed[:own_hidden]
    exp = jnp.transpose(fed[own_hidden:].reshape(2, 2 * own_rows, width), (1, 0, 2)).reshape(2 * own_rows, hidden)
    ebias_sum, sums_two = lax.optimization_barrier((ebias_sum, sums_two, dproj2))[:2]

    def spread(values):
        value = jnp.concatenate(values)
        zero = jnp.zeros_like(value)
        return jnp.where(core == 0, jnp.concatenate([value, zero]), jnp.concatenate([zero, value]))

    pair_sums = (sums_p0[0], sums_p1[0], sums_p2[0])
    owners = 2 * chips
    sums = jnp.stack(
        [spread([p[: 2 * HD] for p in pair_sums]), spread([p[4 * HD :] for p in pair_sums]),
         sums_two[2], sums_two[0], sums_two[1], sums_two[3]]
    )
    sums = jnp.concatenate([sums_one[:2], sums])
    table = jnp.transpose(sums.reshape(8, owners, own_rows), (1, 0, 2)).reshape(owners, 8 * own_rows)
    eb = jnp.where(jnp.arange(2)[None, :, None] == core, ebias_sum.reshape(chips, 1, own_hidden), 0.0)
    table = jnp.concatenate([table, eb.reshape(owners, own_hidden)], axis=1)
    small_sum = pick(reduce_small(table), 2 * chip + core)

    def mine_of(value, target):
        return lax.dynamic_slice_in_dim(value, target * own_rows, own_rows, 0)

    def both(value):
        mine, other = mine_of(value, core), swap(mine_of(value, 1 - core))
        return jnp.where(core == 0, jnp.stack([mine, other]), jnp.stack([other, mine])).astype(f32)

    exp_both, part_both, tail_both = both(exp), both(part), both(tail)
    grad_expand = jnp.transpose(
        exp_both.reshape(2, own_rows, chips, own_hidden), (1, 2, 0, 3)
    ).reshape(own_rows, -1)
    grad_output = jnp.transpose(part_both[:, :, :group], (1, 0, 2)).reshape(own_rows, width)
    grad_project = jnp.concatenate([part_both[:, :, group:], tail_both], axis=2)
    grad_project = jnp.transpose(
        grad_project.reshape(2, own_rows, pairs_dev, 3, 2 * HD), (1, 3, 0, 2, 4)
    ).reshape(own_rows, -1)
    cut = [small_sum[i * own_rows : (i + 1) * own_rows] for i in range(8)]
    return (
        layer_output,
        input_grad,
        cut[0],
        cut[1],
        grad_project,
        cut[2],
        cut[3],
        grad_output,
        cut[4],
        cut[5],
        cut[6],
        grad_expand,
        small_sum[8 * own_rows : 8 * own_rows + own_hidden],
        red.astype(f32),
        cut[7],
    )


def solution(mesh):
    owners, groups = mesh.shape["fsdp"], mesh.shape["sp"]
    split = Mesh(mesh.devices.reshape(owners // 2, 2, groups), ("chip", "core", "sp"))
    own = ("chip", "core")
    rows, flat, both = P(own, None), P(own), P(own, "sp", None)
    return jax.shard_map(
        layer,
        mesh=split,
        in_specs=(both, P(own, "sp"), flat, flat, rows, flat, flat, rows, flat, flat, flat, rows, flat,
                  rows, flat, both),
        out_specs=(both, both, flat, flat, rows, flat, flat, rows, flat, flat, flat, rows, flat, rows, flat),
        check_vma=False,
    )
```
